256 devices in a mesh: seq: 64 (over y, x_lo, z), head: 4 (over x_hi, core).
Axes of the slice: x: 4 (x_hi: 2, x_lo: 2; x = x_hi * 2 + x_lo), y: 4, z: 8, core: 2. Of those that a mesh axis runs over, the one named last changes fastest.
Arguments:
- query_raw: bfloat16 [32768, 4096], P('seq', 'head'), may hold values from -600 to 600
- key_before_norm: bfloat16 [32768, 2048], P('seq', 'head'), may hold values from -600 to 600
- value_input: bfloat16 [32768, 2048], P('seq', 'head'), may hold values from -6 to 6
- out_cotangent: bfloat16 [32768, 4096], P('seq', 'head'), may hold values from -6 to 6
- query_gain: float32 [128], replicated, may hold values from 0.5 to 7
- key_norm_gain: float32 [128], replicated, may hold values from 0.5 to 7
- doc_starts: int32 [4, 8], replicated, may hold values from 0 to 8191, as said below
- windows: int32 [4], replicated, may hold values from 513 to 1024, as said below
Outputs:
- query_gradient: bfloat16 [32768, 4096], P('seq', 'head')
- key_gradient: bfloat16 [32768, 2048], P('seq', 'head')
- value_gradient: bfloat16 [32768, 2048], P('seq', 'head')
- query_norm_gain_gradient: float32 [128], replicated
- key_norm_gain_gradient: float32 [128], replicated
The draws below stay inside these ranges and needn't reach their ends.
Inputs may be any that keep to these rules, and one draw needn't show every extreme that they name: `doc_starts`: each row begins with 0 and rises strictly; no document starts at position 4096. `windows`: some sequence has a window of exactly 1024.
All inputs are finite; a program needn't handle non-finite values.
Results may differ from the reference program's by a relative error of at most 0.025.
The reference program's roundings to bfloat16 on the way count: a program that leaves them out, or rounds other values in their place, can miss the bound.
Values may be sent and summed in bfloat16 or wider, within the bound.
A program may use at most 128 MiB of HBM per device.

```python
import math
import jax
import jax.numpy as jnp
from jax import lax

QUERY_HEADS = 32
KEY_VALUE_HEADS = 16
HEAD_SIZE = 128
WINDOW = 1024
TOKENS_PER_SHARD = 512
SLABS = 4
DOCS = 8
TOTAL_TOKENS = 32768
LENGTH = 8192


def scaled_gaussian(key, count_rows, columns):
    noise_key, row_key, column_key = jax.random.split(key, 3)
    noise_rows = jnp.clip(jax.random.normal(noise_key, (count_rows, columns), jnp.float32), -6.0, 6.0)
    row_scale = jnp.exp(jax.random.uniform(row_key, (count_rows, 1), jnp.float32, 0.0, math.log(10.0)))
    column_scale = jnp.exp(jax.random.uniform(column_key, (1, columns), jnp.float32, 0.0, math.log(10.0)))
    return noise_rows * row_scale * column_scale


def key_provider(key):
    return scaled_gaussian(jax.random.fold_in(key, 11), TOTAL_TOKENS, KEY_VALUE_HEADS * HEAD_SIZE)


def draw_key_before_norm(key, part):
    return key_provider(key).astype(jnp.bfloat16)


def draw_query_raw(key, part):
    values = scaled_gaussian(jax.random.fold_in(key, 23), TOTAL_TOKENS, QUERY_HEADS * HEAD_SIZE)
    return values.astype(jnp.bfloat16)


def draw_query_gain(key, part):
    gain_key = jax.random.fold_in(key, 41)
    return jax.random.uniform(gain_key, (HEAD_SIZE,), jnp.float32, 0.5, 2.0)


def draw_key_norm_gain(key, part):
    gain_key = jax.random.fold_in(key, 43)
    return jax.random.uniform(gain_key, (HEAD_SIZE,), jnp.float32, 0.5, 2.0)


def slab_starts(slab_key):
    picked = jax.random.permutation(slab_key, LENGTH - 2)[:DOCS - 1].astype(jnp.int32) + 1
    picked = jnp.where(picked >= LENGTH // 2, picked + 1, picked)
    return jnp.sort(picked)


def draw_doc_starts(key, part):
    keys_list = jax.random.split(jax.random.fold_in(key, 53), SLABS)
    inner = jax.vmap(slab_starts)(keys_list)
    inner = inner.at[0, DOCS - 2].set(LENGTH - 1)
    return jnp.concatenate([jnp.zeros((SLABS, 1), jnp.int32), inner], axis=1).astype(jnp.int32)


def draw_windows(key, part):
    width_key, slot_key = jax.random.split(jax.random.fold_in(key, 61))
    widths = jax.random.randint(width_key, (SLABS,), WINDOW // 2 + 1, WINDOW + 1)
    chosen = jax.random.randint(slot_key, (), 0, SLABS)
    return jnp.where(jnp.arange(SLABS) == chosen, WINDOW, widths).astype(jnp.int32)


def shard_levels(key, dims, cuts, least, largest):
    level, own = 1.0, jax.random.fold_in(key, 6)
    for dim, parts in cuts:
        draws = jnp.exp(jax.random.uniform(jax.random.fold_in(own, dim), (parts,), jnp.float32, least / len(cuts), largest / len(cuts)))
        level = level * jnp.repeat(draws, dims[dim] // parts).reshape([-1 if axis == dim else 1 for axis in range(len(dims))])
    return level


def gaussian(key, dims, scale, limit, pieces=(), kind=jnp.bfloat16):
    factor_of = shard_levels(key, dims, pieces, -0.22, 0.18) if pieces else 1.0
    values = jax.random.normal(key, dims, jnp.float32) * scale * factor_of
    return jnp.minimum(jnp.maximum(values, -limit), limit).astype(kind)


def setup_inputs(seed: int = 0) -> dict:
    seeds = jax.random.split(jax.random.key(seed), 9)
    return {
        "query_raw": draw_query_raw(jax.random.fold_in(seeds[8], 71), 0),
        "key_before_norm": draw_key_before_norm(jax.random.fold_in(seeds[8], 71), 0),
        "value_input": gaussian(seeds[2], (TOTAL_TOKENS, KEY_VALUE_HEADS * HEAD_SIZE), 1.0, 6.0, ((0, 64), (1, 4))),
        "out_cotangent": gaussian(seeds[3], (TOTAL_TOKENS, QUERY_HEADS * HEAD_SIZE), 1.0, 6.0, ((0, 64), (1, 4))),
        "query_gain": draw_query_gain(jax.random.fold_in(seeds[8], 71), 0),
        "key_norm_gain": draw_key_norm_gain(jax.random.fold_in(seeds[8], 71), 0),
        "doc_starts": draw_doc_starts(jax.random.fold_in(seeds[8], 71), 0),
        "windows": draw_windows(jax.random.fold_in(seeds[8], 71), 0),
    }


score_scale = 168.0 ** (-0.5)
norm_eps = 1e-06
masked_score = -1e+30

def token_info(token_ids, doc_starts, windows, slab_length, total_tokens):
    placed = (token_ids + total_tokens - slab_length // 2) % total_tokens
    slab_id = placed // slab_length
    in_slab = placed - slab_id * slab_length
    one_hot = (jnp.arange(windows.shape[0], dtype=jnp.int32)[None, :] == slab_id[:, None]).astype(jnp.int32)
    row_starts = lax.optimization_barrier(jnp.sum(one_hot[:, :, None] * doc_starts[None, :, :], axis=1))
    reached = row_starts <= in_slab[:, None]
    doc_count = lax.optimization_barrier(jnp.sum(reached.astype(jnp.int32), axis=1))
    doc_begin = lax.optimization_barrier(jnp.max(jnp.where(reached, row_starts, 0), axis=1))
    doc_id = slab_id * doc_starts.shape[1] + doc_count
    win_size = lax.optimization_barrier(jnp.sum(one_hot * windows[None, :], axis=1))
    return (doc_id, in_slab, in_slab - doc_begin, win_size)

def rope_tables(rope_pos, head_dim):
    half_dim = head_dim // 2
    spacing = jnp.arange(half_dim, dtype=jnp.float32) * (2.0 / head_dim)
    inverse_freq = 10000.0 ** (-spacing)
    angle = rope_pos.astype(jnp.float32)[:, None] * inverse_freq[None, :]
    return (jnp.cos(angle)[:, None, :], jnp.sin(angle)[:, None, :])

def apply_norm(raw_rows, gain_vec, cosine_table, sine_table):
    floats = raw_rows.astype(jnp.float32)
    inverse = lax.rsqrt(lax.optimization_barrier(jnp.mean(floats * floats, axis=-1)) + norm_eps)
    scaled = floats * inverse[..., None] * gain_vec
    half_dim = scaled.shape[-1] // 2
    low_half, high_half = (scaled[..., :half_dim], scaled[..., half_dim:])
    turned = jnp.concatenate([low_half * cosine_table - high_half * sine_table, high_half * cosine_table + low_half * sine_table], axis=-1)
    return (turned.astype(jnp.bfloat16), floats, inverse)

def norm_backward(grad_hat, floats, inverse, gain_vec, cosine_table, sine_table):
    half_dim = grad_hat.shape[-1] // 2
    low_half, high_half = (grad_hat[..., :half_dim], grad_hat[..., half_dim:])
    grad_scaled = jnp.concatenate([low_half * cosine_table + high_half * sine_table, high_half * cosine_table - low_half * sine_table], axis=-1)
    unit_rows = floats * inverse[..., None]
    gain_grad = lax.optimization_barrier(jnp.sum(grad_scaled * unit_rows, axis=(0, 1)))
    weighted = grad_scaled * gain_vec
    correction = lax.optimization_barrier(jnp.mean(weighted * floats, axis=-1))
    grad_raw = inverse[..., None] * weighted - floats * (inverse * inverse * inverse * correction)[..., None]
    return (grad_raw, gain_grad)

def reference(query_raw, key_before_norm, value_input, out_cotangent, query_gain, key_norm_gain, doc_starts, windows):
    group_width = QUERY_HEADS // KEY_VALUE_HEADS
    reach_shards = (WINDOW - 1) // TOKENS_PER_SHARD + 1
    window_margin = reach_shards * TOKENS_PER_SHARD
    key_span = window_margin + TOKENS_PER_SHARD
    token_ids = jnp.arange(TOTAL_TOKENS, dtype=jnp.int32)
    doc_id, in_slab, rope_pos, win_size = token_info(token_ids, doc_starts, windows, LENGTH, TOTAL_TOKENS)
    cosine_table, sine_table = rope_tables(rope_pos, HEAD_SIZE)
    query_unit, query_float, query_inverse = apply_norm(query_raw.reshape(TOTAL_TOKENS, QUERY_HEADS, HEAD_SIZE), query_gain, cosine_table, sine_table)
    key_unit, key_single, key_inverse_norm = apply_norm(key_before_norm.reshape(TOTAL_TOKENS, KEY_VALUE_HEADS, HEAD_SIZE), key_norm_gain, cosine_table, sine_table)
    value_row_block = value_input.reshape(TOTAL_TOKENS, KEY_VALUE_HEADS, HEAD_SIZE)
    gradient_rows = out_cotangent.reshape(TOTAL_TOKENS, QUERY_HEADS, HEAD_SIZE)
    tail_start = TOTAL_TOKENS - window_margin
    key_with_padding = jnp.concatenate([key_unit[tail_start:], key_unit], 0)
    value_with_padding = jnp.concatenate([value_row_block[tail_start:], value_row_block], 0)
    doc_padded = jnp.concatenate([doc_id[tail_start:], doc_id], 0)
    slab_padded = jnp.concatenate([in_slab[tail_start:], in_slab], 0)

    def block_step(running, block_id):
        key_acc, value_accumulator = running
        first_row = (block_id * TOKENS_PER_SHARD).astype(jnp.int32)
        query_tile = lax.dynamic_slice_in_dim(query_unit, first_row, TOKENS_PER_SHARD, 0).reshape(TOKENS_PER_SHARD, KEY_VALUE_HEADS, group_width, HEAD_SIZE).astype(jnp.float32)
        gradient_block = lax.dynamic_slice_in_dim(gradient_rows, first_row, TOKENS_PER_SHARD, 0).reshape(TOKENS_PER_SHARD, KEY_VALUE_HEADS, group_width, HEAD_SIZE).astype(jnp.float32)
        block_doc = lax.dynamic_slice_in_dim(doc_id, first_row, TOKENS_PER_SHARD, 0)
        block_slab = lax.dynamic_slice_in_dim(in_slab, first_row, TOKENS_PER_SHARD, 0)
        block_window = lax.dynamic_slice_in_dim(win_size, first_row, TOKENS_PER_SHARD, 0)
        key_block = lax.dynamic_slice_in_dim(key_with_padding, first_row, key_span, 0).astype(jnp.float32)
        value_block = lax.dynamic_slice_in_dim(value_with_padding, first_row, key_span, 0).astype(jnp.float32)
        near_doc = lax.dynamic_slice_in_dim(doc_padded, first_row, key_span, 0)
        near_slab = lax.dynamic_slice_in_dim(slab_padded, first_row, key_span, 0)
        pos_gap = block_slab[:, None] - near_slab[None, :]
        visible = (block_doc[:, None] == near_doc[None, :]) & (pos_gap >= 0) & (pos_gap < block_window[:, None])
        scores = jnp.einsum('rhgd,khd->hgrk', query_tile, key_block) * score_scale
        scores = jnp.where(visible[None, None], scores, masked_score)
        row_max = lax.optimization_barrier(jnp.max(scores, axis=-1, keepdims=True))
        exponent = jnp.exp(scores - row_max)
        row_sum = lax.optimization_barrier(jnp.sum(exponent, axis=-1, keepdims=True))
        softmax = exponent / row_sum
        grad_soft = jnp.einsum('rhgd,khd->hgrk', gradient_block, value_block)
        row_delta = lax.optimization_barrier(jnp.sum(softmax * grad_soft, axis=-1, keepdims=True))
        grad_scores = lax.optimization_barrier((softmax * (grad_soft - row_delta)).astype(jnp.bfloat16)).astype(jnp.float32)
        soft_half = lax.optimization_barrier(softmax.astype(jnp.bfloat16)).astype(jnp.float32)
        grad_query = score_scale * jnp.einsum('hgrk,khd->rhgd', grad_scores, key_block)
        grad_key = score_scale * jnp.einsum('hgrk,rhgd->khd', grad_scores, query_tile)
        grad_value = jnp.einsum('hgrk,rhgd->khd', soft_half, gradient_block)
        key_acc = lax.dynamic_update_slice_in_dim(key_acc, lax.dynamic_slice_in_dim(key_acc, first_row, key_span, 0) + grad_key, first_row, 0)
        value_accumulator = lax.dynamic_update_slice_in_dim(value_accumulator, lax.dynamic_slice_in_dim(value_accumulator, first_row, key_span, 0) + grad_value, first_row, 0)
        return ((key_acc, value_accumulator), grad_query.reshape(TOKENS_PER_SHARD, QUERY_HEADS, HEAD_SIZE))
    initial_accumulator = jnp.zeros((TOTAL_TOKENS + window_margin, KEY_VALUE_HEADS, HEAD_SIZE), jnp.float32)
    (key_acc, value_accumulator), grad_query = lax.scan(block_step, (initial_accumulator, initial_accumulator), jnp.arange(TOTAL_TOKENS // TOKENS_PER_SHARD, dtype=jnp.int32))
    grad_query_hat = grad_query.reshape(TOTAL_TOKENS, QUERY_HEADS, HEAD_SIZE)
    grad_key_hat = key_acc[window_margin:].at[tail_start:].add(key_acc[:window_margin])
    value_total = value_accumulator[window_margin:].at[tail_start:].add(value_accumulator[:window_margin])
    query_gradient, query_norm_gain_gradient = norm_backward(grad_query_hat, query_float, query_inverse, query_gain, cosine_table, sine_table)
    key_gradient, key_norm_gain_gradient = norm_backward(grad_key_hat, key_single, key_inverse_norm, key_norm_gain, cosine_table, sine_table)
    value_gradient = value_total.reshape(TOTAL_TOKENS, KEY_VALUE_HEADS * HEAD_SIZE).astype(jnp.bfloat16)
    return (query_gradient.reshape(TOTAL_TOKENS, QUERY_HEADS * HEAD_SIZE).astype(jnp.bfloat16), key_gradient.reshape(TOTAL_TOKENS, KEY_VALUE_HEADS * HEAD_SIZE).astype(jnp.bfloat16), value_gradient, query_norm_gain_gradient, key_norm_gain_gradient)
```

```python
import functools
import math

import jax
import jax.numpy as jnp
from jax import lax
from jax.experimental import pallas as pl
from jax.experimental.pallas import tpu as pltpu
from jax.sharding import PartitionSpec as P

SLABS = 4
ROWS = 512
TILE = 256
SPAN = 1280
KEYS = 1536
DIM = 128
HEADS = 4

score_scale = 168.0 ** (-0.5)
exp2_scale = score_scale * math.log2(math.e)
norm_eps = 1e-06
masked_score = -1e30
f32 = jnp.float32
bf16 = jnp.bfloat16
MESH = pl.DeviceIdType.MESH


def half_turn(x):
    return pltpu.roll(x, DIM // 2, 1)


def unit_rows(raw):
    x = raw.astype(f32)
    inverse = lax.rsqrt(jnp.mean(x * x, axis=-1, keepdims=True) + norm_eps)
    return x * inverse, inverse


def fold_rows(x):
    return jnp.sum(x.reshape(x.shape[0] // 8, 8, DIM), axis=0)


def cos_sin(angle, cos_lane):
    turns = jnp.floor(angle * (2.0 / math.pi) + 0.5)
    rest = angle - turns * 1.5703125
    rest = rest - turns * 4.837512969970703e-4
    rest = rest - turns * 7.549789954891882e-8
    square = rest * rest
    sine = rest + rest * square * (
        -1.6666654611e-1 + square * (8.3321608736e-3 - square * 1.9515295891e-4)
    )
    cosine = 1.0 - 0.5 * square + square * square * (
        4.166664568298827e-2 + square * (-1.388731625493765e-3 + square * 2.443315711809948e-5)
    )
    quarter = turns + jnp.where(cos_lane, 1.0, 0.0)
    quarter = quarter - 4.0 * jnp.floor(quarter * 0.25)
    odd = (quarter == 1.0) | (quarter == 3.0)
    value = jnp.where(odd, cosine, sine)
    return jnp.where(quarter >= 2.0, -value, value)


def kernel(
    shards,
    heads,
    q_hbm,
    k_hbm,
    v_hbm,
    do_hbm,
    query_gain,
    key_gain,
    inverse_freq,
    doc_starts,
    windows,
    dq_hbm,
    dk_hbm,
    dv_hbm,
    gain_out,
    kcat,
    vcat,
    q_all,
    do_all,
    cos_table,
    sin_table,
    khat,
    kunit,
    qhat,
    qunit,
    qinv,
    dos,
    scores,
    soft_grad,
    acc_k,
    acc_v,
    far_send,
    far_in,
    near_send,
    near_in,
    dq_all,
    dk_all,
    dv_all,
    gain_acc,
    sum_send,
    sum_in,
    local_sem,
    out_sem,
    fwd_send,
    fwd_recv,
    relay_send,
    relay_recv,
    far_ssem,
    far_rsem,
    near_ssem,
    near_rsem,
    sum_ssem,
    sum_rsem,
):
    total = shards * ROWS
    length = total // SLABS
    me = lax.axis_index("seq")
    my_head = lax.axis_index("head")
    ahead = lax.rem(me + 1, shards)
    behind = lax.rem(me + shards - 1, shards)
    low_size = min(8, shards)
    high_size = shards // low_size
    my_low = lax.rem(me, low_size)
    my_high = me // low_size
    stages = [
        (heads, my_head, lambda n: (me, n)),
        (low_size, my_low, lambda n: (my_high * low_size + n, my_head)),
        (high_size, my_high, lambda n: (n * low_size + my_low, my_head)),
    ]

    barrier = pltpu.get_barrier_semaphore()
    pl.semaphore_signal(barrier, inc=1, device_id=(ahead, my_head), device_id_type=MESH)
    pl.semaphore_signal(barrier, inc=1, device_id=(behind, my_head), device_id_type=MESH)
    greeted = 2
    for size, mine, place in stages:
        for k in range(1, size):
            pl.semaphore_signal(
                barrier,
                inc=1,
                device_id=place(lax.rem(mine + k, size)),
                device_id_type=MESH,
            )
            greeted += 1
    pl.semaphore_wait(barrier, greeted)

    def columns(j, width=DIM):
        return pl.ds(pl.multiple_of(j * width, width), width)

    def own_copies(j):
        return [
            pltpu.make_async_remote_copy(
                src_ref=src.at[:, columns(j)],
                dst_ref=dst.at[j, pl.ds(ROWS, ROWS), :],
                send_sem=fwd_send.at[j, n],
                recv_sem=fwd_recv.at[j, n],
                device_id=(ahead, my_head),
                device_id_type=MESH,
            )
            for n, (src, dst) in enumerate(((k_hbm, kcat), (v_hbm, vcat)))
        ]

    def relay_copies(j):
        return [
            pltpu.make_async_remote_copy(
                src_ref=buf.at[j, pl.ds(ROWS, ROWS), :],
                dst_ref=buf.at[j, pl.ds(0, ROWS), :],
                send_sem=relay_send.at[j, n],
                recv_sem=relay_recv.at[j, n],
                device_id=(ahead, my_head),
                device_id_type=MESH,
            )
            for n, buf in enumerate((kcat, vcat))
        ]

    def back_copies(j, src, dst, ssem, rsem):
        return [
            pltpu.make_async_remote_copy(
                src_ref=src.at[j, n],
                dst_ref=dst.at[j, n],
                send_sem=ssem.at[j, n],
                recv_sem=rsem.at[j, n],
                device_id=(behind, my_head),
                device_id_type=MESH,
            )
            for n in range(2)
        ]

    def far_copies(j):
        return back_copies(j, far_send, far_in, far_ssem, far_rsem)

    def near_copies(j):
        return back_copies(j, near_send, near_in, near_ssem, near_rsem)

    def start_own(j):
        for copy in own_copies(j):
            copy.start()

    def relay(j):
        for arrived, onward in zip(own_copies(j), relay_copies(j)):
            arrived.wait_recv()
            onward.start()

    start_own(0)
    start_own(1)
    local = []
    for j in range(HEADS):
        local.append((k_hbm.at[:, columns(j)], kcat.at[j, pl.ds(2 * ROWS, ROWS), :]))
        local.append((v_hbm.at[:, columns(j)], vcat.at[j, pl.ds(2 * ROWS, ROWS), :]))
    local.append((q_hbm, q_all))
    local.append((do_hbm, do_all))
    local = [
        pltpu.make_async_copy(src, dst, local_sem.at[n]) for n, (src, dst) in enumerate(local)
    ]
    for copy in local:
        copy.start()

    def block_info(block):
        shard = lax.rem(me + shards - 2 + block, shards)
        placed = lax.rem(shard * ROWS + total - length // 2, total)
        slab = placed // length
        return slab, placed - slab * length

    def rope_position(in_slab, slab):
        begin = jnp.zeros_like(in_slab)
        for n in range(doc_starts.shape[1]):
            start = doc_starts[slab, n]
            begin = jnp.where(in_slab >= start, jnp.maximum(begin, start), begin)
        return in_slab - begin

    lane = lax.broadcasted_iota(jnp.int32, (TILE, DIM), 1)
    cos_lane = lane < DIM // 2

    def table_step(n, carry):
        block = n // (ROWS // TILE)
        slab, first = block_info(block)
        offset = lax.rem(n, ROWS // TILE) * TILE
        in_slab = first + offset + lax.broadcasted_iota(jnp.int32, (TILE, DIM), 0)
        position = rope_position(in_slab, slab).astype(f32)
        both = cos_sin(position * inverse_freq[...], cos_lane)
        other = half_turn(both)
        here = pl.ds(pl.multiple_of(n * TILE, TILE), TILE)
        cos_table[here, :] = jnp.where(cos_lane, both, other)
        sin_table[here, :] = jnp.where(cos_lane, -other, both)
        return carry

    lax.fori_loop(0, KEYS // TILE, table_step, 0)
    gain_acc[...] = jnp.zeros_like(gain_acc)

    relay(0)
    start_own(2)
    for copy in local:
        copy.wait()

    slab, first = block_info(2)
    window = windows[slab]

    def key_norm(j, start, count):
        def step(n, carry):
            here = pl.ds(pl.multiple_of(start + n * TILE, TILE), TILE)
            unit, _ = unit_rows(kcat[j, here, :])
            scaled = unit * key_gain[...]
            khat[here, :] = (
                scaled * cos_table[here, :] + half_turn(scaled) * sin_table[here, :]
            ).astype(bf16)
            kunit[here, :] = unit
            return carry

        lax.fori_loop(0, count // TILE, step, 0)

    nt = (((1,), (1,)), ((), ()))
    nn = (((1,), (0,)), ((), ()))
    tn = (((0,), (0,)), ((), ()))

    def attend(j, i):
        base = i * TILE
        rows = pl.ds(pl.multiple_of(base, TILE), TILE)
        mine = pl.ds(pl.multiple_of(base + 2 * ROWS, TILE), TILE)
        for g in range(2):
            head_columns = pl.ds(pl.multiple_of((2 * j + g) * DIM, DIM), DIM)
            part = pl.ds(g * TILE, TILE)
            unit, inverse = unit_rows(q_all[rows, head_columns])
            scaled = unit * query_gain[...]
            qhat[part, :] = (
                scaled * cos_table[mine, :] + half_turn(scaled) * sin_table[mine, :]
            ).astype(bf16)
            qunit[part, :] = unit
            qinv[part, :] = jnp.broadcast_to(inverse, (TILE, DIM))
            dos[part, :] = do_all[rows, head_columns]
        q = qhat[...]
        out_grad = dos[...]

        row = lax.rem(lax.broadcasted_iota(jnp.int32, (1, 2 * TILE), 1), TILE)
        in_slab = first + base + row
        reach = jnp.minimum(rope_position(in_slab, slab), window - 1)
        lowest = 2 * ROWS + row - reach
        key_row = lax.broadcasted_iota(jnp.int32, (TILE, 2 * TILE), 0)

        row_max = jnp.full((1, 2 * TILE), masked_score, f32)
        for t in range(SPAN // TILE):
            keys = khat[pl.ds(pl.multiple_of(base + t * TILE, TILE), TILE), :]
            tile = lax.dot_general(keys, q, nt, preferred_element_type=f32)
            visible = key_row >= lowest - t * TILE
            if t == SPAN // TILE - 1:
                visible = visible & (key_row <= row)
            tile = jnp.where(visible, tile, masked_score)
            scores[pl.ds(t * TILE, TILE), :] = tile
            row_max = jnp.maximum(row_max, jnp.max(tile, axis=0, keepdims=True))
        shift = row_max * exp2_scale
        row_sum = jnp.zeros((1, 2 * TILE), f32)
        delta = jnp.zeros((1, 2 * TILE), f32)
        for t in range(SPAN // TILE):
            here = pl.ds(t * TILE, TILE)
            values = vcat[j, pl.ds(pl.multiple_of(base + t * TILE, TILE), TILE), :]
            gradient = lax.dot_general(values, out_grad, nt, preferred_element_type=f32)
            exponent = jnp.exp2(scores[here, :] * exp2_scale - shift)
            row_sum += jnp.sum(exponent, axis=0, keepdims=True)
            delta += jnp.sum(exponent * gradient, axis=0, keepdims=True)
            scores[here, :] = exponent
            soft_grad[here, :] = gradient
        inverse_sum = 1.0 / row_sum
        delta = delta * inverse_sum
        query_grad = jnp.zeros((2 * TILE, DIM), f32)
        for t in range(SPAN // TILE):
            here = pl.ds(t * TILE, TILE)
            there = pl.ds(pl.multiple_of(base + t * TILE, TILE), TILE)
            softmax = scores[here, :] * inverse_sum
            grad_scores = (softmax * (soft_grad[here, :] - delta)).astype(bf16)
            acc_v[j, there, :] += lax.dot_general(
                softmax.astype(bf16), out_grad, nn, preferred_element_type=f32
            )
            acc_k[j, there, :] += lax.dot_general(
                grad_scores, q, nn, preferred_element_type=f32
            )
            query_grad += lax.dot_general(
                grad_scores, khat[there, :], tn, preferred_element_type=f32
            )
        for g in range(2):
            head_columns = pl.ds(pl.multiple_of((2 * j + g) * DIM, DIM), DIM)
            part = pl.ds(g * TILE, TILE)
            grad = query_grad[g * TILE : (g + 1) * TILE] * score_scale
            turned = grad * cos_table[mine, :] - half_turn(grad) * sin_table[mine, :]
            unit = qunit[part, :]
            gain_acc[0] += fold_rows(turned * unit)
            weighted = turned * query_gain[...]
            mean = jnp.mean(weighted * unit, axis=-1, keepdims=True)
            dq_all[rows, head_columns] = (qinv[part, :] * (weighted - unit * mean)).astype(bf16)

    def dq_copy(j):
        return pltpu.make_async_copy(
            dq_all.at[:, columns(j, 2 * DIM)], dq_hbm.at[:, columns(j, 2 * DIM)], out_sem.at[j, 0]
        )

    def dk_copy(j):
        return pltpu.make_async_copy(
            dk_all.at[:, columns(j)], dk_hbm.at[:, columns(j)], out_sem.at[j, 1]
        )

    def dv_copy(j):
        return pltpu.make_async_copy(
            dv_all.at[:, columns(j)], dv_hbm.at[:, columns(j)], out_sem.at[j, 2]
        )

    def hand_on(j):
        for n, (copy, onward, acc) in enumerate(
            zip(far_copies(j), near_copies(j), (acc_k, acc_v))
        ):
            copy.wait_recv()
            near_send[j, n] = (
                far_in[j, n].astype(f32) + acc[j, pl.ds(ROWS, ROWS), :]
            ).astype(bf16)
            onward.start()

    def finish(j):
        key_copy, value_copy = near_copies(j)
        key_copy.wait_recv()

        def key_step(n, carry):
            rows = pl.ds(pl.multiple_of(n * TILE, TILE), TILE)
            mine = pl.ds(pl.multiple_of(2 * ROWS + n * TILE, TILE), TILE)
            grad = (near_in[j, 0, rows, :].astype(f32) + acc_k[j, mine, :]) * score_scale
            turned = grad * cos_table[mine, :] - half_turn(grad) * sin_table[mine, :]
            unit, inverse = unit_rows(kcat[j, mine, :])
            weighted = turned * key_gain[...]
            mean = jnp.mean(weighted * unit, axis=-1, keepdims=True)
            dk_all[rows, columns(j)] = (inverse * (weighted - unit * mean)).astype(bf16)
            return carry

        lax.fori_loop(0, ROWS // TILE, key_step, 0)
        dk_copy(j).start()
        value_copy.wait_recv()

        def value_step(n, carry):
            rows = pl.ds(pl.multiple_of(n * TILE, TILE), TILE)
            mine = pl.ds(pl.multiple_of(2 * ROWS + n * TILE, TILE), TILE)
            dv_all[rows, columns(j)] = (
                near_in[j, 1, rows, :].astype(f32) + acc_v[j, mine, :]
            ).astype(bf16)
            return carry

        lax.fori_loop(0, ROWS // TILE, value_step, 0)
        dv_copy(j).start()

    def head_step(j, carry):
        key_norm(j, ROWS, 2 * ROWS)
        acc_k[j] = jnp.zeros((KEYS, DIM), f32)
        acc_v[j] = jnp.zeros((KEYS, DIM), f32)

        @pl.when(j < HEADS - 1)
        def _():
            relay(j + 1)

        @pl.when(j < HEADS - 3)
        def _():
            start_own(j + 3)

        for copy in relay_copies(j):
            copy.wait_recv()
        key_norm(j, 0, ROWS)

        def row_step(i, inner):
            attend(j, i)
            return inner

        lax.fori_loop(0, ROWS // TILE, row_step, 0)
        far_send[j, 0] = acc_k[j, pl.ds(0, ROWS), :].astype(bf16)
        far_send[j, 1] = acc_v[j, pl.ds(0, ROWS), :].astype(bf16)
        for copy in far_copies(j):
            copy.start()
        dq_copy(j).start()

        def gain_step(n, inner):
            here = pl.ds(pl.multiple_of(n * TILE, TILE), TILE)
            grad = acc_k[j, here, :] * score_scale
            turned = grad * cos_table[here, :] - half_turn(grad) * sin_table[here, :]
            gain_acc[1] += fold_rows(turned * kunit[here, :])
            return inner

        lax.fori_loop(0, KEYS // TILE, gain_step, 0)

        @pl.when(j >= 1)
        def _():
            hand_on(j - 1)

        @pl.when(j >= 2)
        def _():
            finish(j - 2)

        return carry

    lax.fori_loop(0, HEADS, head_step, 0)

    def sum_copy(n, k):
        size, mine, place = stages[n]
        return pltpu.make_async_remote_copy(
            src_ref=sum_send.at[n],
            dst_ref=sum_in.at[n, mine],
            send_sem=sum_ssem.at[n, k],
            recv_sem=sum_rsem.at[n, mine],
            device_id=place(lax.rem(mine + k, size)),
            device_id_type=MESH,
        )

    def sum_arrival(n, k):
        size, mine, place = stages[n]
        source = lax.rem(mine + size - k, size)
        return pltpu.make_async_remote_copy(
            src_ref=sum_send.at[n],
            dst_ref=sum_in.at[n, source],
            send_sem=sum_ssem.at[n, k],
            recv_sem=sum_rsem.at[n, source],
            device_id=place(source),
            device_id_type=MESH,
        )

    def start_sum(n, value):
        size, mine, place = stages[n]
        sum_send[n] = value
        sum_in[n, mine] = value
        for k in range(1, size):
            sum_copy(n, k).start()

    def end_sum(n):
        size, mine, place = stages[n]
        for k in range(1, size):
            sum_arrival(n, k).wait_recv()
        value = sum_in[n, 0]
        for k in range(1, size):
            value = value + sum_in[n, k]
        return value

    spread = jnp.where(
        lax.broadcasted_iota(jnp.int32, (8, DIM), 0) == 0,
        jnp.sum(gain_acc[0], axis=0, keepdims=True),
        jnp.sum(gain_acc[1], axis=0, keepdims=True),
    )
    start_sum(0, spread)
    hand_on(HEADS - 1)
    start_sum(1, end_sum(0))
    finish(HEADS - 2)
    start_sum(2, end_sum(1))
    gain_out[...] = end_sum(2)
    finish(HEADS - 1)

    for n, (size, mine, place) in enumerate(stages):
        for k in range(1, size):
            sum_copy(n, k).wait_send()

    def drain(j, carry):
        for copies in (own_copies(j), relay_copies(j), far_copies(j), near_copies(j)):
            for copy in copies:
                copy.wait_send()
        dq_copy(j).wait()
        dk_copy(j).wait()
        dv_copy(j).wait()
        return carry

    lax.fori_loop(0, HEADS, drain, 0)


def solution(mesh):
    shards, heads = mesh.shape["seq"], mesh.shape["head"]
    most = max(heads, 8, shards // 8)

    def step(q, k, v, out_grad, query_gain, key_gain, doc_starts, windows):
        spacing = jnp.arange(DIM // 2, dtype=f32) * (2.0 / DIM)
        inverse_freq = 10000.0 ** (-spacing)
        inverse_freq = jnp.concatenate([inverse_freq, inverse_freq])[None]
        hbm = pl.BlockSpec(memory_space=pl.ANY)
        vmem = pl.BlockSpec(memory_space=pltpu.VMEM)
        smem = pl.BlockSpec(memory_space=pltpu.SMEM)
        dq, dk, dv, gains = pl.pallas_call(
            functools.partial(kernel, shards, heads),
            out_shape=(
                jax.ShapeDtypeStruct(q.shape, bf16),
                jax.ShapeDtypeStruct(k.shape, bf16),
                jax.ShapeDtypeStruct(v.shape, bf16),
                jax.ShapeDtypeStruct((8, DIM), f32),
            ),
            in_specs=[hbm] * 4 + [vmem] * 3 + [smem] * 2,
            out_specs=(hbm, hbm, hbm, vmem),
            scratch_shapes=[
                pltpu.VMEM((HEADS, KEYS, DIM), bf16),
                pltpu.VMEM((HEADS, KEYS, DIM), bf16),
                pltpu.VMEM((ROWS, 2 * HEADS * DIM), bf16),
                pltpu.VMEM((ROWS, 2 * HEADS * DIM), bf16),
                pltpu.VMEM((KEYS, DIM), f32),
                pltpu.VMEM((KEYS, DIM), f32),
                pltpu.VMEM((KEYS, DIM), bf16),
                pltpu.VMEM((KEYS, DIM), f32),
                pltpu.VMEM((2 * TILE, DIM), bf16),
                pltpu.VMEM((2 * TILE, DIM), f32),
                pltpu.VMEM((2 * TILE, DIM), f32),
                pltpu.VMEM((2 * TILE, DIM), bf16),
                pltpu.VMEM((SPAN, 2 * TILE), f32),
                pltpu.VMEM((SPAN, 2 * TILE), f32),
                pltpu.VMEM((HEADS, KEYS, DIM), f32),
                pltpu.VMEM((HEADS, KEYS, DIM), f32),
                pltpu.VMEM((HEADS, 2, ROWS, DIM), bf16),
                pltpu.VMEM((HEADS, 2, ROWS, DIM), bf16),
                pltpu.VMEM((HEADS, 2, ROWS, DIM), bf16),
                pltpu.VMEM((HEADS, 2, ROWS, DIM), bf16),
                pltpu.VMEM((ROWS, 2 * HEADS * DIM), bf16),
                pltpu.VMEM((ROWS, HEADS * DIM), bf16),
                pltpu.VMEM((ROWS, HEADS * DIM), bf16),
                pltpu.VMEM((2, 8, DIM), f32),
                pltpu.VMEM((3, 8, DIM), f32),
                pltpu.VMEM((3, most, 8, DIM), f32),
                pltpu.SemaphoreType.DMA((2 * HEADS + 2,)),
                pltpu.SemaphoreType.DMA((HEADS, 3)),
            ]
            + [pltpu.SemaphoreType.DMA((HEADS, 2)) for _ in range(8)]
            + [pltpu.SemaphoreType.DMA((3, most)) for _ in range(2)],
            compiler_params=pltpu.CompilerParams(
                collective_id=0, has_side_effects=True, vmem_limit_bytes=60 * 1024 * 1024
            ),
        )(
            q,
            k,
            v,
            out_grad,
            query_gain[None],
            key_gain[None],
            inverse_freq,
            doc_starts,
            windows,
        )
        return dq, dk, dv, gains[0], gains[1]

    split = P("seq", "head")
    return jax.shard_map(
        step,
        mesh=mesh,
        in_specs=(split,) * 4 + (P(),) * 4,
        out_specs=(split, split, split, P(), P()),
        check_vma=False,
    )
```

```python
import functools
import math

import jax
import jax.numpy as jnp
from jax import lax
from jax.experimental import pallas as pl
from jax.experimental.pallas import tpu as pltpu
from jax.sharding import PartitionSpec as P

SLABS = 4
ROWS = 512
TILE = 256
SPAN = 1280
KEYS = 1536
DIM = 128
HEADS = 4

score_scale = 168.0 ** (-0.5)
exp2_scale = score_scale * math.log2(math.e)
norm_eps = 1e-06
masked_score = -1e30
f32 = jnp.float32
bf16 = jnp.bfloat16
MESH = pl.DeviceIdType.MESH


def half_turn(x):
    return pltpu.roll(x, DIM // 2, 1)


def unit_rows(raw):
    x = raw.astype(f32)
    inverse = lax.rsqrt(jnp.mean(x * x, axis=-1, keepdims=True) + norm_eps)
    return x * inverse, inverse


def fold_rows(x):
    return jnp.sum(x.reshape(x.shape[0] // 8, 8, DIM), axis=0)


def cos_sin(angle, cos_lane):
    turns = jnp.floor(angle * (2.0 / math.pi) + 0.5)
    rest = angle - turns * 1.5703125
    rest = rest - turns * 4.837512969970703e-4
    rest = rest - turns * 7.549789954891882e-8
    square = rest * rest
    sine = rest + rest * square * (
        -1.6666654611e-1 + square * (8.3321608736e-3 - square * 1.9515295891e-4)
    )
    cosine = 1.0 - 0.5 * square + square * square * (
        4.166664568298827e-2 + square * (-1.388731625493765e-3 + square * 2.443315711809948e-5)
    )
    quarter = turns + jnp.where(cos_lane, 1.0, 0.0)
    quarter = quarter - 4.0 * jnp.floor(quarter * 0.25)
    odd = (quarter == 1.0) | (quarter == 3.0)
    value = jnp.where(odd, cosine, sine)
    return jnp.where(quarter >= 2.0, -value, value)


def kernel(
    shards,
    heads,
    q_hbm,
    k_hbm,
    v_hbm,
    do_hbm,
    query_gain,
    key_gain,
    inverse_freq,
    doc_starts,
    windows,
    dq_all,
    dk_all,
    dv_all,
    query_gain_out,
    key_gain_out,
    kcat,
    vcat,
    q_all,
    do_all,
    cos_table,
    sin_table,
    khat,
    kunit,
    qhat,
    qunit,
    qinv,
    dos,
    scores,
    soft_grad,
    acc_k,
    acc_v,
    far_send,
    far_in,
    near_send,
    near_in,
    gain_acc,
    sum_send,
    sum_in,
    local_sem,
    fwd_send,
    fwd_recv,
    relay_send,
    relay_recv,
    far_ssem,
    far_rsem,
    near_ssem,
    near_rsem,
    sum_ssem,
    sum_rsem,
):
    total = shards * ROWS
    length = total // SLABS
    me = lax.axis_index("seq")
    my_head = lax.axis_index("head")
    ahead = lax.rem(me + 1, shards)
    behind = lax.rem(me + shards - 1, shards)
    low_size = min(8, shards)
    high_size = shards // low_size
    my_low = lax.rem(me, low_size)
    my_high = me // low_size
    stages = [
        (heads, my_head, lambda n: (me, n)),
        (low_size, my_low, lambda n: (my_high * low_size + n, my_head)),
        (high_size, my_high, lambda n: (n * low_size + my_low, my_head)),
    ]

    barrier = pltpu.get_barrier_semaphore()
    pl.semaphore_signal(barrier, inc=1, device_id=(ahead, my_head), device_id_type=MESH)
    pl.semaphore_signal(barrier, inc=1, device_id=(behind, my_head), device_id_type=MESH)
    greeted = 2
    for size, mine, place in stages:
        for k in range(1, size):
            pl.semaphore_signal(
                barrier,
                inc=1,
                device_id=place(lax.rem(mine + k, size)),
                device_id_type=MESH,
            )
            greeted += 1
    pl.semaphore_wait(barrier, greeted)

    def columns(j, width=DIM):
        return pl.ds(pl.multiple_of(j * width, width), width)

    def own_copies(j, which=(0, 1)):
        return [
            pltpu.make_async_remote_copy(
                src_ref=src.at[:, columns(j)],
                dst_ref=dst.at[j, pl.ds(ROWS, ROWS), :],
                send_sem=fwd_send.at[j, n],
                recv_sem=fwd_recv.at[j, n],
                device_id=(ahead, my_head),
                device_id_type=MESH,
            )
            for n, (src, dst) in enumerate(((k_hbm, kcat), (v_hbm, vcat)))
            if n in which
        ]

    def relay_copies(j, which=(0, 1)):
        return [
            pltpu.make_async_remote_copy(
                src_ref=buf.at[j, pl.ds(ROWS, ROWS), :],
                dst_ref=buf.at[j, pl.ds(0, ROWS), :],
                send_sem=relay_send.at[j, n],
                recv_sem=relay_recv.at[j, n],
                device_id=(ahead, my_head),
                device_id_type=MESH,
            )
            for n, buf in enumerate((kcat, vcat))
            if n in which
        ]

    def back_copies(j, src, dst, ssem, rsem):
        return [
            pltpu.make_async_remote_copy(
                src_ref=src.at[j, n],
                dst_ref=dst.at[j, n],
                send_sem=ssem.at[j, n],
                recv_sem=rsem.at[j, n],
                device_id=(behind, my_head),
                device_id_type=MESH,
            )
            for n in range(2)
        ]

    def far_copies(j):
        return back_copies(j, far_send, far_in, far_ssem, far_rsem)

    def near_copies(j):
        return back_copies(j, near_send, near_in, near_ssem, near_rsem)

    def start_own(j, n):
        own_copies(j, (n,))[0].start()

    def relay(j, n):
        own_copies(j, (n,))[0].wait_recv()
        relay_copies(j, (n,))[0].start()

    start_own(0, 0)
    start_own(0, 1)
    start_own(1, 0)
    local = []
    for j in range(HEADS):
        local.append((k_hbm.at[:, columns(j)], kcat.at[j, pl.ds(2 * ROWS, ROWS), :]))
        local.append((v_hbm.at[:, columns(j)], vcat.at[j, pl.ds(2 * ROWS, ROWS), :]))
    local.append((q_hbm, q_all))
    local.append((do_hbm, do_all))
    local = [
        pltpu.make_async_copy(src, dst, local_sem.at[n]) for n, (src, dst) in enumerate(local)
    ]
    for copy in local:
        copy.start()

    def block_info(block):
        shard = lax.rem(me + shards - 2 + block, shards)
        placed = lax.rem(shard * ROWS + total - length // 2, total)
        slab = placed // length
        return slab, placed - slab * length

    def rope_position(in_slab, slab):
        begin = jnp.zeros_like(in_slab)
        for n in range(doc_starts.shape[1]):
            start = doc_starts[slab, n]
            begin = jnp.where(in_slab >= start, jnp.maximum(begin, start), begin)
        return in_slab - begin

    lane = lax.broadcasted_iota(jnp.int32, (TILE, DIM), 1)
    cos_lane = lane < DIM // 2

    def table_step(n, carry):
        block = n // (ROWS // TILE)
        slab, first = block_info(block)
        offset = lax.rem(n, ROWS // TILE) * TILE
        in_slab = first + offset + lax.broadcasted_iota(jnp.int32, (TILE, DIM), 0)
        position = rope_position(in_slab, slab).astype(f32)
        both = cos_sin(position * inverse_freq[...], cos_lane)
        other = half_turn(both)
        here = pl.ds(pl.multiple_of(n * TILE, TILE), TILE)
        cos_table[here, :] = jnp.where(cos_lane, both, other)
        sin_table[here, :] = jnp.where(cos_lane, -other, both)
        return carry

    lax.fori_loop(0, KEYS // TILE, table_step, 0)
    gain_acc[...] = jnp.zeros_like(gain_acc)

    for copy in local:
        copy.wait()
    relay(0, 0)
    relay(0, 1)
    start_own(1, 1)
    start_own(2, 0)
    relay(1, 0)

    slab, first = block_info(2)
    window = windows[slab]

    def key_norm(j, start, count):
        def step(n, carry):
            here = pl.ds(pl.multiple_of(start + n * TILE, TILE), TILE)
            unit, _ = unit_rows(kcat[j, here, :])
            scaled = unit * key_gain[...]
            khat[here, :] = (
                scaled * cos_table[here, :] + half_turn(scaled) * sin_table[here, :]
            ).astype(bf16)
            kunit[here, :] = unit
            return carry

        lax.fori_loop(0, count // TILE, step, 0)

    nt = (((1,), (1,)), ((), ()))
    nn = (((1,), (0,)), ((), ()))
    tn = (((0,), (0,)), ((), ()))

    def attend(j, i):
        base = i * TILE
        rows = pl.ds(pl.multiple_of(base, TILE), TILE)
        mine = pl.ds(pl.multiple_of(base + 2 * ROWS, TILE), TILE)
        for g in range(2):
            head_columns = pl.ds(pl.multiple_of((2 * j + g) * DIM, DIM), DIM)
            part = pl.ds(g * TILE, TILE)
            unit, inverse = unit_rows(q_all[rows, head_columns])
            scaled = unit * query_gain[...]
            qhat[part, :] = (
                scaled * cos_table[mine, :] + half_turn(scaled) * sin_table[mine, :]
            ).astype(bf16)
            qunit[part, :] = unit
            qinv[part, :] = jnp.broadcast_to(inverse, (TILE, DIM))
            dos[part, :] = do_all[rows, head_columns]
        row = lax.broadcasted_iota(jnp.int32, (1, TILE), 1)
        in_slab = first + base + row
        reach = jnp.minimum(rope_position(in_slab, slab), window - 1)
        lowest = 2 * ROWS + row - reach
        key_row = lax.broadcasted_iota(jnp.int32, (TILE, TILE), 0)
        q = [qhat[pl.ds(g * TILE, TILE), :] for g in range(2)]
        out_grad = [dos[pl.ds(g * TILE, TILE), :] for g in range(2)]
        row_max = [jnp.full((1, TILE), masked_score, f32)] * 2
        row_sum = [jnp.zeros((1, TILE), f32)] * 2
        delta = [jnp.zeros((1, TILE), f32)] * 2
        query_grad = [jnp.zeros((DIM, TILE), f32)] * 2
        tiles = SPAN // TILE

        def there(t):
            return pl.ds(pl.multiple_of(base + t * TILE, TILE), TILE)

        def here(t):
            return pl.ds(t * TILE, TILE)

        def score_tile(g, t):
            tile = lax.dot_general(khat[there(t), :], q[g], nt, preferred_element_type=f32)
            visible = key_row >= lowest - t * TILE
            if t == tiles - 1:
                visible = visible & (key_row <= row)
            tile = jnp.where(visible, tile, masked_score)
            scores[g, here(t), :] = tile
            row_max[g] = jnp.maximum(row_max[g], jnp.max(tile, axis=0, keepdims=True))

        def gradient_tile(g, t):
            soft_grad[g, here(t), :] = lax.dot_general(
                vcat[j, there(t), :], out_grad[g], nt, preferred_element_type=f32
            )

        def exponent_tile(g, t):
            exponent = jnp.exp2(scores[g, here(t), :] * exp2_scale - row_max[g])
            row_sum[g] = row_sum[g] + jnp.sum(exponent, axis=0, keepdims=True)
            delta[g] = delta[g] + jnp.sum(
                exponent * soft_grad[g, here(t), :], axis=0, keepdims=True
            )
            scores[g, here(t), :] = exponent

        def product_tile(g, t):
            softmax = scores[g, here(t), :] * row_sum[g]
            grad_scores = (softmax * (soft_grad[g, here(t), :] - delta[g])).astype(bf16)
            acc_v[j, there(t), :] += lax.dot_general(
                softmax.astype(bf16), out_grad[g], nn, preferred_element_type=f32
            )
            acc_k[j, there(t), :] += lax.dot_general(
                grad_scores, q[g], nn, preferred_element_type=f32
            )
            query_grad[g] = query_grad[g] + lax.dot_general(
                khat[there(t), :], grad_scores, tn, preferred_element_type=f32
            )

        def close_max(g):
            row_max[g] = row_max[g] * exp2_scale

        def close_sum(g):
            row_sum[g] = 1.0 / row_sum[g]
            delta[g] = delta[g] * row_sum[g]

        for t in range(tiles):
            score_tile(0, t)
        for t in range(tiles):
            gradient_tile(0, t)
        close_max(0)
        for t in range(tiles):
            score_tile(1, t)
            exponent_tile(0, t)
        close_max(1)
        close_sum(0)
        for t in range(tiles):
            gradient_tile(1, t)
            product_tile(0, t)
            exponent_tile(1, t)
        close_sum(1)
        for t in range(tiles):
            product_tile(1, t)
        for g in range(2):
            head_columns = pl.ds(pl.multiple_of((2 * j + g) * DIM, DIM), DIM)
            part = pl.ds(g * TILE, TILE)
            grad = query_grad[g].T * score_scale
            turned = grad * cos_table[mine, :] - half_turn(grad) * sin_table[mine, :]
            unit = qunit[part, :]
            gain_acc[0] += fold_rows(turned * unit)
            weighted = turned * query_gain[...]
            mean = jnp.mean(weighted * unit, axis=-1, keepdims=True)
            dq_all[rows, head_columns] = (qinv[part, :] * (weighted - unit * mean)).astype(bf16)

    def hand_on(j):
        for n, (copy, onward, acc) in enumerate(
            zip(far_copies(j), near_copies(j), (acc_k, acc_v))
        ):
            copy.wait_recv()
            near_send[j, n] = (
                far_in[j, n].astype(f32) + acc[j, pl.ds(ROWS, ROWS), :]
            ).astype(bf16)
            onward.start()

    def finish(j):
        key_copy, value_copy = near_copies(j)
        key_copy.wait_recv()

        def key_step(n, carry):
            rows = pl.ds(pl.multiple_of(n * TILE, TILE), TILE)
            mine = pl.ds(pl.multiple_of(2 * ROWS + n * TILE, TILE), TILE)
            grad = (near_in[j, 0, rows, :].astype(f32) + acc_k[j, mine, :]) * score_scale
            turned = grad * cos_table[mine, :] - half_turn(grad) * sin_table[mine, :]
            unit, inverse = unit_rows(kcat[j, mine, :])
            weighted = turned * key_gain[...]
            mean = jnp.mean(weighted * unit, axis=-1, keepdims=True)
            dk_all[rows, columns(j)] = (inverse * (weighted - unit * mean)).astype(bf16)
            return carry

        lax.fori_loop(0, ROWS // TILE, key_step, 0)
        value_copy.wait_recv()

        def value_step(n, carry):
            rows = pl.ds(pl.multiple_of(n * TILE, TILE), TILE)
            mine = pl.ds(pl.multiple_of(2 * ROWS + n * TILE, TILE), TILE)
            dv_all[rows, columns(j)] = (
                near_in[j, 1, rows, :].astype(f32) + acc_v[j, mine, :]
            ).astype(bf16)
            return carry

        lax.fori_loop(0, ROWS // TILE, value_step, 0)

    def between(j):
        @pl.when(j == 0)
        def _():
            relay(1, 1)
            start_own(2, 1)
            start_own(3, 0)

        @pl.when(j == 1)
        def _():
            relay(2, 1)
            start_own(3, 1)
            hand_on(0)

        @pl.when(j == 2)
        def _():
            relay(3, 1)
            finish(0)

    def head_step(j, carry):
        key_norm(j, ROWS, 2 * ROWS)
        acc_k[j] = jnp.zeros((KEYS, DIM), f32)
        acc_v[j] = jnp.zeros((KEYS, DIM), f32)
        for copy in relay_copies(j):
            copy.wait_recv()
        key_norm(j, 0, ROWS)

        def row_step(i, inner):
            attend(j, i)

            @pl.when(i == 0)
            def _():
                between(j)

            return inner

        lax.fori_loop(0, ROWS // TILE, row_step, 0)
        far_send[j, 0] = acc_k[j, pl.ds(0, ROWS), :].astype(bf16)
        far_send[j, 1] = acc_v[j, pl.ds(0, ROWS), :].astype(bf16)
        for copy in far_copies(j):
            copy.start()

        @pl.when(j < 2)
        def _():
            relay(j + 2, 0)

        def gain_step(n, inner):
            here = pl.ds(pl.multiple_of(n * TILE, TILE), TILE)
            grad = acc_k[j, here, :] * score_scale
            turned = grad * cos_table[here, :] - half_turn(grad) * sin_table[here, :]
            gain_acc[1] += fold_rows(turned * kunit[here, :])
            return inner

        lax.fori_loop(0, KEYS // TILE, gain_step, 0)

        @pl.when(j == 2)
        def _():
            hand_on(1)

        return carry

    lax.fori_loop(0, HEADS, head_step, 0)

    def sum_copy(n, k):
        size, mine, place = stages[n]
        return pltpu.make_async_remote_copy(
            src_ref=sum_send.at[n],
            dst_ref=sum_in.at[n, mine],
            send_sem=sum_ssem.at[n, k],
            recv_sem=sum_rsem.at[n, mine],
            device_id=place(lax.rem(mine + k, size)),
            device_id_type=MESH,
        )

    def sum_arrival(n, k):
        size, mine, place = stages[n]
        source = lax.rem(mine + size - k, size)
        return pltpu.make_async_remote_copy(
            src_ref=sum_send.at[n],
            dst_ref=sum_in.at[n, source],
            send_sem=sum_ssem.at[n, k],
            recv_sem=sum_rsem.at[n, source],
            device_id=place(source),
            device_id_type=MESH,
        )

    def start_sum(n, value):
        size, mine, place = stages[n]
        sum_send[n] = value
        sum_in[n, mine] = value
        for k in range(1, size):
            sum_copy(n, k).start()

    def end_sum(n):
        size, mine, place = stages[n]
        for k in range(1, size):
            sum_arrival(n, k).wait_recv()
        value = sum_in[n, 0]
        for k in range(1, size):
            value = value + sum_in[n, k]
        return value

    spread = jnp.where(
        lax.broadcasted_iota(jnp.int32, (8, DIM), 0) == 0,
        jnp.sum(gain_acc[0], axis=0, keepdims=True),
        jnp.sum(gain_acc[1], axis=0, keepdims=True),
    )
    start_sum(0, spread)
    hand_on(2)
    finish(1)
    start_sum(1, end_sum(0))
    hand_on(3)
    start_sum(2, end_sum(1))
    finish(2)
    gains = end_sum(2)
    query_gain_out[...] = gains[0:1]
    key_gain_out[...] = gains[1:2]
    finish(3)

    for n, (size, mine, place) in enumerate(stages):
        for k in range(1, size):
            sum_copy(n, k).wait_send()

    def drain(j, carry):
        for copies in (own_copies(j), relay_copies(j), far_copies(j), near_copies(j)):
            for copy in copies:
                copy.wait_send()
        return carry

    lax.fori_loop(0, HEADS, drain, 0)


def solution(mesh):
    shards, heads = mesh.shape["seq"], mesh.shape["head"]
    most = max(heads, 8, shards // 8)

    def step(q, k, v, out_grad, query_gain, key_gain, doc_starts, windows):
        spacing = jnp.arange(DIM // 2, dtype=f32) * (2.0 / DIM)
        inverse_freq = 10000.0 ** (-spacing)
        inverse_freq = jnp.concatenate([inverse_freq, inverse_freq])[None]
        hbm = pl.BlockSpec(memory_space=pltpu.HBM)
        vmem = pl.BlockSpec(memory_space=pltpu.VMEM)
        smem = pl.BlockSpec(memory_space=pltpu.SMEM)
        dq, dk, dv, dq_gain, dk_gain = pl.pallas_call(
            functools.partial(kernel, shards, heads),
            out_shape=(
                pltpu.VMEM(q.shape, bf16),
                pltpu.VMEM(k.shape, bf16),
                pltpu.VMEM(v.shape, bf16),
                pltpu.VMEM((1, DIM), f32),
                pltpu.VMEM((1, DIM), f32),
            ),
            in_specs=[hbm] * 4 + [vmem] * 3 + [smem] * 2,
            out_specs=(vmem,) * 5,
            scratch_shapes=[
                pltpu.VMEM((HEADS, KEYS, DIM), bf16),
                pltpu.VMEM((HEADS, KEYS, DIM), bf16),
                pltpu.VMEM((ROWS, 2 * HEADS * DIM), bf16),
                pltpu.VMEM((ROWS, 2 * HEADS * DIM), bf16),
                pltpu.VMEM((KEYS, DIM), f32),
                pltpu.VMEM((KEYS, DIM), f32),
                pltpu.VMEM((KEYS, DIM), bf16),
                pltpu.VMEM((KEYS, DIM), f32),
                pltpu.VMEM((2 * TILE, DIM), bf16),
                pltpu.VMEM((2 * TILE, DIM), f32),
                pltpu.VMEM((2 * TILE, DIM), f32),
                pltpu.VMEM((2 * TILE, DIM), bf16),
                pltpu.VMEM((2, SPAN, TILE), f32),
                pltpu.VMEM((2, SPAN, TILE), f32),
                pltpu.VMEM((HEADS, KEYS, DIM), f32),
                pltpu.VMEM((HEADS, KEYS, DIM), f32),
                pltpu.VMEM((HEADS, 2, ROWS, DIM), bf16),
                pltpu.VMEM((HEADS, 2, ROWS, DIM), bf16),
                pltpu.VMEM((HEADS, 2, ROWS, DIM), bf16),
                pltpu.VMEM((HEADS, 2, ROWS, DIM), bf16),
                pltpu.VMEM((2, 8, DIM), f32),
                pltpu.VMEM((3, 8, DIM), f32),
                pltpu.VMEM((3, most, 8, DIM), f32),
                pltpu.SemaphoreType.DMA((2 * HEADS + 2,)),
            ]
            + [pltpu.SemaphoreType.DMA((HEADS, 2)) for _ in range(8)]
            + [pltpu.SemaphoreType.DMA((3, most)) for _ in range(2)],
            compiler_params=pltpu.CompilerParams(
                collective_id=0, has_side_effects=True, vmem_limit_bytes=58 * 1024 * 1024
            ),
        )(
            q,
            k,
            v,
            out_grad,
            query_gain[None],
            key_gain[None],
            inverse_freq,
            doc_starts,
            windows,
        )
        return dq, dk, dv, dq_gain[0], dk_gain[0]

    split = P("seq", "head")
    return jax.shard_map(
        step,
        mesh=mesh,
        in_specs=(split,) * 4 + (P(),) * 4,
        out_specs=(split, split, split, P(), P()),
        check_vma=False,
    )
```

```python
import functools
import math

import jax
import jax.numpy as jnp
import numpy as np
from jax import lax
from jax.experimental import pallas as pl
from jax.experimental.pallas import tpu as pltpu
from jax.sharding import PartitionSpec as P

SLABS = 4
ROWS = 512
TILE = 256
SPAN = 1280
KEYS = 1536
DIM = 128
HEADS = 4

score_scale = 168.0 ** (-0.5)
exp2_scale = score_scale * math.log2(math.e)
norm_eps = 1e-06
masked_score = -1e30
f32 = jnp.float32
bf16 = jnp.bfloat16
MESH = pl.DeviceIdType.MESH


def half_turn(x):
    return pltpu.roll(x, DIM // 2, 1)


def unit_rows(raw):
    x = raw.astype(f32)
    inverse = lax.rsqrt(jnp.mean(x * x, axis=-1, keepdims=True) + norm_eps)
    return x * inverse, inverse


def fold_rows(x):
    return jnp.sum(x.reshape(x.shape[0] // 8, 8, DIM), axis=0)


def cos_sin(angle, cos_lane):
    turns = jnp.floor(angle * (2.0 / math.pi) + 0.5)
    rest = angle - turns * 1.5703125
    rest = rest - turns * 4.837512969970703e-4
    rest = rest - turns * 7.549789954891882e-8
    square = rest * rest
    sine = rest + rest * square * (
        -1.6666654611e-1 + square * (8.3321608736e-3 - square * 1.9515295891e-4)
    )
    cosine = 1.0 - 0.5 * square + square * square * (
        4.166664568298827e-2 + square * (-1.388731625493765e-3 + square * 2.443315711809948e-5)
    )
    quarter = turns + jnp.where(cos_lane, 1.0, 0.0)
    quarter = quarter - 4.0 * jnp.floor(quarter * 0.25)
    odd = (quarter == 1.0) | (quarter == 3.0)
    value = jnp.where(odd, cosine, sine)
    return jnp.where(quarter >= 2.0, -value, value)


def kernel(
    shards,
    heads,
    q_hbm,
    k_hbm,
    v_hbm,
    do_hbm,
    query_gain,
    key_gain,
    inverse_freq,
    doc_starts,
    windows,
    dq_all,
    dk_all,
    dv_all,
    query_gain_out,
    key_gain_out,
    kcat,
    vcat,
    q_all,
    do_all,
    cos_table,
    sin_table,
    khat,
    kunit,
    qhat,
    qunit,
    qinv,
    dos,
    scores,
    soft_grad,
    acc_k,
    acc_v,
    far_send,
    far_in,
    near_send,
    near_in,
    gain_acc,
    sum_send,
    sum_in,
    local_sem,
    fwd_send,
    fwd_recv,
    relay_send,
    relay_recv,
    far_ssem,
    far_rsem,
    near_ssem,
    near_rsem,
    sum_ssem,
    sum_rsem,
):
    total = shards * ROWS
    length = total // SLABS
    me = lax.axis_index("seq")
    my_head = lax.axis_index("head")
    ahead = lax.rem(me + 1, shards)
    behind = lax.rem(me + shards - 1, shards)
    low_size = min(8, shards)
    high_size = shards // low_size
    my_low = lax.rem(me, low_size)
    my_high = me // low_size
    stages = [
        (low_size, my_low, lambda n: (my_high * low_size + n, my_head)),
        (heads, my_head, lambda n: (me, n)),
        (high_size, my_high, lambda n: (n * low_size + my_low, my_head)),
    ]

    barrier = pltpu.get_barrier_semaphore()
    pl.semaphore_signal(barrier, inc=1, device_id=(ahead, my_head), device_id_type=MESH)
    pl.semaphore_signal(barrier, inc=1, device_id=(behind, my_head), device_id_type=MESH)
    greeted = 2
    for size, mine, place in stages:
        for k in range(1, size):
            pl.semaphore_signal(
                barrier,
                inc=1,
                device_id=place(lax.rem(mine + k, size)),
                device_id_type=MESH,
            )
            greeted += 1
    pl.semaphore_wait(barrier, greeted)

    def columns(j, width=DIM):
        return pl.ds(pl.multiple_of(j * width, width), width)

    def own_copies(j, which=(0, 1)):
        return [
            pltpu.make_async_remote_copy(
                src_ref=src.at[:, columns(j)],
                dst_ref=dst.at[j, pl.ds(ROWS, ROWS), :],
                send_sem=fwd_send.at[j, n],
                recv_sem=fwd_recv.at[j, n],
                device_id=(ahead, my_head),
                device_id_type=MESH,
            )
            for n, (src, dst) in enumerate(((k_hbm, kcat), (v_hbm, vcat)))
            if n in which
        ]

    def relay_copies(j, which=(0, 1)):
        return [
            pltpu.make_async_remote_copy(
                src_ref=buf.at[j, pl.ds(ROWS, ROWS), :],
                dst_ref=buf.at[j, pl.ds(0, ROWS), :],
                send_sem=relay_send.at[j, n],
                recv_sem=relay_recv.at[j, n],
                device_id=(ahead, my_head),
                device_id_type=MESH,
            )
            for n, buf in enumerate((kcat, vcat))
            if n in which
        ]

    def back_copies(j, half, which, src, dst, ssem, rsem):
        rows = pl.ds(pl.multiple_of(half * TILE, TILE), TILE)
        return [
            pltpu.make_async_remote_copy(
                src_ref=src.at[j, n, rows, :],
                dst_ref=dst.at[j, n, rows, :],
                send_sem=ssem.at[j, n, half],
                recv_sem=rsem.at[j, n, half],
                device_id=(behind, my_head),
                device_id_type=MESH,
            )
            for n in which
        ]

    def far_copies(j, half, which=(0, 1)):
        return back_copies(j, half, which, far_send, far_in, far_ssem, far_rsem)

    def near_copies(j, half, which=(0, 1)):
        return back_copies(j, half, which, near_send, near_in, near_ssem, near_rsem)

    def start_own(j, n):
        own_copies(j, (n,))[0].start()

    def relay(j, n):
        own_copies(j, (n,))[0].wait_recv()
        relay_copies(j, (n,))[0].start()

    start_own(0, 0)
    start_own(0, 1)
    start_own(1, 0)
    local = []
    for j in range(HEADS):
        local.append((k_hbm.at[:, columns(j)], kcat.at[j, pl.ds(2 * ROWS, ROWS), :]))
        local.append((v_hbm.at[:, columns(j)], vcat.at[j, pl.ds(2 * ROWS, ROWS), :]))
    local.append((q_hbm, q_all))
    local.append((do_hbm, do_all))
    local = [
        pltpu.make_async_copy(src, dst, local_sem.at[n]) for n, (src, dst) in enumerate(local)
    ]
    for copy in local:
        copy.start()

    def block_info(block):
        shard = lax.rem(me + shards - 2 + block, shards)
        placed = lax.rem(shard * ROWS + total - length // 2, total)
        slab = placed // length
        return slab, placed - slab * length

    def rope_position(in_slab, slab):
        begin = jnp.zeros_like(in_slab)
        for n in range(doc_starts.shape[1]):
            start = doc_starts[slab, n]
            begin = jnp.where(in_slab >= start, jnp.maximum(begin, start), begin)
        return in_slab - begin

    lane = lax.broadcasted_iota(jnp.int32, (TILE, DIM), 1)
    cos_lane = lane < DIM // 2

    def table_step(n, carry):
        block = n // (ROWS // TILE)
        slab, first = block_info(block)
        offset = lax.rem(n, ROWS // TILE) * TILE
        in_slab = first + offset + lax.broadcasted_iota(jnp.int32, (TILE, DIM), 0)
        position = rope_position(in_slab, slab).astype(f32)
        both = cos_sin(position * inverse_freq[...], cos_lane)
        other = half_turn(both)
        here = pl.ds(pl.multiple_of(n * TILE, TILE), TILE)
        cos_table[here, :] = jnp.where(cos_lane, both, other)
        sin_table[here, :] = jnp.where(cos_lane, -other, both)
        return carry

    lax.fori_loop(0, KEYS // TILE, table_step, 0)
    gain_acc[...] = jnp.zeros_like(gain_acc)

    for copy in local:
        copy.wait()
    relay(0, 0)
    relay(0, 1)
    start_own(1, 1)
    start_own(2, 0)
    relay(1, 0)

    slab, first = block_info(2)
    window = windows[slab]

    def key_norm(j, start, count):
        def step(n, carry):
            here = pl.ds(pl.multiple_of(start + n * TILE, TILE), TILE)
            unit, _ = unit_rows(kcat[j, here, :])
            scaled = unit * key_gain[...]
            khat[here, :] = (
                scaled * cos_table[here, :] + half_turn(scaled) * sin_table[here, :]
            ).astype(bf16)
            kunit[here, :] = unit
            return carry

        lax.fori_loop(0, count // TILE, step, 0)

    nt = (((1,), (1,)), ((), ()))
    nn = (((1,), (0,)), ((), ()))
    tn = (((0,), (0,)), ((), ()))

    def attend(j, i):
        base = i * TILE
        rows = pl.ds(pl.multiple_of(base, TILE), TILE)
        mine = pl.ds(pl.multiple_of(base + 2 * ROWS, TILE), TILE)
        for g in range(2):
            head_columns = pl.ds(pl.multiple_of((2 * j + g) * DIM, DIM), DIM)
            part = pl.ds(g * TILE, TILE)
            unit, inverse = unit_rows(q_all[rows, head_columns])
            scaled = unit * query_gain[...]
            qhat[part, :] = (
                scaled * cos_table[mine, :] + half_turn(scaled) * sin_table[mine, :]
            ).astype(bf16)
            qunit[part, :] = unit
            qinv[part, :] = jnp.broadcast_to(inverse, (TILE, DIM))
            dos[part, :] = do_all[rows, head_columns]
        row = lax.broadcasted_iota(jnp.int32, (1, TILE), 1)
        in_slab = first + base + row
        reach = jnp.minimum(rope_position(in_slab, slab), window - 1)
        lowest = 2 * ROWS + row - reach
        key_row = lax.broadcasted_iota(jnp.int32, (TILE, TILE), 0)
        q = [qhat[pl.ds(g * TILE, TILE), :] for g in range(2)]
        out_grad = [dos[pl.ds(g * TILE, TILE), :] for g in range(2)]
        row_max = [jnp.full((1, TILE), masked_score, f32)] * 2
        row_sum = [jnp.zeros((1, TILE), f32)] * 2
        delta = [jnp.zeros((1, TILE), f32)] * 2
        query_grad = [jnp.zeros((DIM, TILE), f32)] * 2
        tiles = SPAN // TILE

        def there(t):
            return pl.ds(pl.multiple_of(base + t * TILE, TILE), TILE)

        def here(t):
            return pl.ds(t * TILE, TILE)

        def score_tile(g, t):
            tile = lax.dot_general(khat[there(t), :], q[g], nt, preferred_element_type=f32)
            visible = key_row >= lowest - t * TILE
            if t == tiles - 1:
                visible = visible & (key_row <= row)
            tile = jnp.where(visible, tile, masked_score)
            scores[g, here(t), :] = tile
            row_max[g] = jnp.maximum(row_max[g], jnp.max(tile, axis=0, keepdims=True))

        def gradient_tile(g, t):
            soft_grad[g, here(t), :] = lax.dot_general(
                vcat[j, there(t), :], out_grad[g], nt, preferred_element_type=f32
            )

        def exponent_tile(g, t):
            exponent = jnp.exp2(scores[g, here(t), :] * exp2_scale - row_max[g])
            row_sum[g] = row_sum[g] + jnp.sum(exponent, axis=0, keepdims=True)
            delta[g] = delta[g] + jnp.sum(
                exponent * soft_grad[g, here(t), :], axis=0, keepdims=True
            )
            scores[g, here(t), :] = exponent

        def product_tile(g, t):
            softmax = scores[g, here(t), :] * row_sum[g]
            grad_scores = (softmax * (soft_grad[g, here(t), :] - delta[g])).astype(bf16)
            acc_v[j, there(t), :] += lax.dot_general(
                softmax.astype(bf16), out_grad[g], nn, preferred_element_type=f32
            )
            acc_k[j, there(t), :] += lax.dot_general(
                grad_scores, q[g], nn, preferred_element_type=f32
            )
            query_grad[g] = query_grad[g] + lax.dot_general(
                khat[there(t), :], grad_scores, tn, preferred_element_type=f32
            )

        def close_max(g):
            row_max[g] = row_max[g] * exp2_scale

        def close_sum(g):
            row_sum[g] = 1.0 / row_sum[g]
            delta[g] = delta[g] * row_sum[g]

        for t in range(tiles):
            score_tile(0, t)
        for t in range(tiles):
            gradient_tile(0, t)
        close_max(0)
        for t in range(tiles):
            score_tile(1, t)
            exponent_tile(0, t)
        close_max(1)
        close_sum(0)
        for t in range(tiles):
            gradient_tile(1, t)
            product_tile(0, t)
            exponent_tile(1, t)
        close_sum(1)
        for t in range(tiles):
            product_tile(1, t)
        for g in range(2):
            head_columns = pl.ds(pl.multiple_of((2 * j + g) * DIM, DIM), DIM)
            part = pl.ds(g * TILE, TILE)
            grad = query_grad[g].T * score_scale
            turned = grad * cos_table[mine, :] - half_turn(grad) * sin_table[mine, :]
            unit = qunit[part, :]
            gain_acc[0] += fold_rows(turned * unit)
            weighted = turned * query_gain[...]
            mean = jnp.mean(weighted * unit, axis=-1, keepdims=True)
            dq_all[rows, head_columns] = (qinv[part, :] * (weighted - unit * mean)).astype(bf16)

    def hand_on(j, half):
        rows = pl.ds(half * TILE, TILE)
        for n, acc in enumerate((acc_k, acc_v)):
            far_copies(j, half, (n,))[0].wait_recv()
            near_send[j, n, rows, :] = (
                far_in[j, n, rows, :].astype(f32) + acc[j, pl.ds(ROWS + half * TILE, TILE), :]
            ).astype(bf16)
            near_copies(j, half, (n,))[0].start()

    def finish(j, half):
        rows = pl.ds(half * TILE, TILE)
        mine = pl.ds(2 * ROWS + half * TILE, TILE)
        unit, inverse = unit_rows(kcat[j, mine, :])
        near_copies(j, half, (0,))[0].wait_recv()
        grad = (near_in[j, 0, rows, :].astype(f32) + acc_k[j, mine, :]) * score_scale
        turned = grad * cos_table[mine, :] - half_turn(grad) * sin_table[mine, :]
        weighted = turned * key_gain[...]
        mean = jnp.mean(weighted * unit, axis=-1, keepdims=True)
        dk_all[rows, columns(j)] = (inverse * (weighted - unit * mean)).astype(bf16)
        near_copies(j, half, (1,))[0].wait_recv()
        dv_all[rows, columns(j)] = (
            near_in[j, 1, rows, :].astype(f32) + acc_v[j, mine, :]
        ).astype(bf16)

    def between(j):
        @pl.when(j < 3)
        def _():
            relay(j + 1, 1)

        @pl.when(j < 2)
        def _():
            start_own(j + 2, 1)

        @pl.when(j == 0)
        def _():
            start_own(3, 0)

        @pl.when(j >= 1)
        def _():
            hand_on(j - 1, 1)

        @pl.when(j == 2)
        def _():
            finish(0, 0)
            finish(0, 1)

    def sum_copy(n, k):
        size, mine, place = stages[n]
        return pltpu.make_async_remote_copy(
            src_ref=sum_send.at[n],
            dst_ref=sum_in.at[n, mine],
            send_sem=sum_ssem.at[n, k],
            recv_sem=sum_rsem.at[n, mine],
            device_id=place(lax.rem(mine + k, size)),
            device_id_type=MESH,
        )

    def sum_arrival(n, k):
        size, mine, place = stages[n]
        source = lax.rem(mine + size - k, size)
        return pltpu.make_async_remote_copy(
            src_ref=sum_send.at[n],
            dst_ref=sum_in.at[n, source],
            send_sem=sum_ssem.at[n, k],
            recv_sem=sum_rsem.at[n, source],
            device_id=place(source),
            device_id_type=MESH,
        )

    def start_sum(n, value):
        size, mine, place = stages[n]
        sum_send[n] = value
        sum_in[n, mine] = value
        for k in range(1, size):
            sum_copy(n, k).start()

    def end_sum(n):
        size, mine, place = stages[n]
        for k in range(1, size):
            sum_arrival(n, k).wait_recv()
        value = sum_in[n, 0]
        for k in range(1, size):
            value = value + sum_in[n, k]
        return value

    def gain_part(j):
        def gain_step(n, inner):
            here = pl.ds(pl.multiple_of(n * TILE, TILE), TILE)
            grad = acc_k[j, here, :] * score_scale
            turned = grad * cos_table[here, :] - half_turn(grad) * sin_table[here, :]
            gain_acc[1] += fold_rows(turned * kunit[here, :])
            return inner

        lax.fori_loop(0, KEYS // TILE, gain_step, 0)

    def last_gain(j):
        gain_part(j)
        spread = jnp.where(
            lax.broadcasted_iota(jnp.int32, (8, DIM), 0) == 0,
            jnp.sum(gain_acc[0], axis=0, keepdims=True),
            jnp.sum(gain_acc[1], axis=0, keepdims=True),
        )
        start_sum(0, spread)

    def head_step(j, carry):
        @pl.when(j >= 1)
        def _():
            hand_on(j - 1, 0)

        key_norm(j, ROWS, 2 * ROWS)
        acc_k[j] = jnp.zeros((KEYS, DIM), f32)
        acc_v[j] = jnp.zeros((KEYS, DIM), f32)
        for copy in relay_copies(j):
            copy.wait_recv()
        key_norm(j, 0, ROWS)

        def row_step(i, inner):
            attend(j, i)

            @pl.when(2 * j + i == 2 * HEADS - 1)
            def _():
                last_gain(j)

            rows = pl.ds(pl.multiple_of(i * TILE, TILE), TILE)
            far_send[j, 0, rows, :] = acc_k[j, rows, :].astype(bf16)
            far_send[j, 1, rows, :] = acc_v[j, rows, :].astype(bf16)
            for copy in far_copies(j, i):
                copy.start()

            @pl.when(i == 0)
            def _():
                between(j)

            return inner

        lax.fori_loop(0, ROWS // TILE, row_step, 0)

        @pl.when(j < 2)
        def _():
            relay(j + 2, 0)

        @pl.when(j < 3)
        def _():
            gain_part(j)

        return carry

    lax.fori_loop(0, HEADS, head_step, 0)

    hand_on(3, 0)
    finish(1, 0)
    finish(1, 1)
    start_sum(1, end_sum(0))
    hand_on(3, 1)
    start_sum(2, end_sum(1))
    finish(2, 0)
    finish(2, 1)
    finish(3, 0)
    gains = end_sum(2)
    query_gain_out[...] = gains[0:1]
    key_gain_out[...] = gains[1:2]
    finish(3, 1)

    for n, (size, mine, place) in enumerate(stages):
        for k in range(1, size):
            sum_copy(n, k).wait_send()

    def drain(j, carry):
        backward = [copy(j, half) for copy in (far_copies, near_copies) for half in range(2)]
        for copies in (own_copies(j), relay_copies(j), *backward):
            for copy in copies:
                copy.wait_send()
        return carry

    lax.fori_loop(0, HEADS, drain, 0)


def write_out(*refs):
    sources, targets, sem = refs[:5], refs[5:10], refs[10]
    copies = [
        pltpu.make_async_copy(src, dst, sem.at[n])
        for n, (src, dst) in enumerate(zip(sources, targets))
    ]
    for copy in copies:
        copy.start()
    for copy in copies:
        copy.wait()


def solution(mesh):
    shards, heads = mesh.shape["seq"], mesh.shape["head"]
    most = max(heads, 8, shards // 8)

    def step(q, k, v, out_grad, query_gain, key_gain, doc_starts, windows):
        inverse_freq = 10000.0 ** (-np.arange(DIM // 2, dtype=np.float64) * (2.0 / DIM))
        inverse_freq = jnp.asarray(np.tile(inverse_freq, 2)[None], f32)
        hbm = pl.BlockSpec(memory_space=pltpu.HBM)
        vmem = pl.BlockSpec(memory_space=pltpu.VMEM)
        smem = pl.BlockSpec(memory_space=pltpu.SMEM)
        results = pl.pallas_call(
            functools.partial(kernel, shards, heads),
            out_shape=(
                pltpu.VMEM(q.shape, bf16),
                pltpu.VMEM(k.shape, bf16),
                pltpu.VMEM(v.shape, bf16),
                pltpu.VMEM((1, DIM), f32),
                pltpu.VMEM((1, DIM), f32),
            ),
            in_specs=[hbm] * 4 + [vmem] * 3 + [smem] * 2,
            out_specs=(vmem,) * 5,
            scratch_shapes=[
                pltpu.VMEM((HEADS, KEYS, DIM), bf16),
                pltpu.VMEM((HEADS, KEYS, DIM), bf16),
                pltpu.VMEM((ROWS, 2 * HEADS * DIM), bf16),
                pltpu.VMEM((ROWS, 2 * HEADS * DIM), bf16),
                pltpu.VMEM((KEYS, DIM), f32),
                pltpu.VMEM((KEYS, DIM), f32),
                pltpu.VMEM((KEYS, DIM), bf16),
                pltpu.VMEM((KEYS, DIM), f32),
                pltpu.VMEM((2 * TILE, DIM), bf16),
                pltpu.VMEM((2 * TILE, DIM), f32),
                pltpu.VMEM((2 * TILE, DIM), f32),
                pltpu.VMEM((2 * TILE, DIM), bf16),
                pltpu.VMEM((2, SPAN, TILE), f32),
                pltpu.VMEM((2, SPAN, TILE), f32),
                pltpu.VMEM((HEADS, KEYS, DIM), f32),
                pltpu.VMEM((HEADS, KEYS, DIM), f32),
                pltpu.VMEM((HEADS, 2, ROWS, DIM), bf16),
                pltpu.VMEM((HEADS, 2, ROWS, DIM), bf16),
                pltpu.VMEM((HEADS, 2, ROWS, DIM), bf16),
                pltpu.VMEM((HEADS, 2, ROWS, DIM), bf16),
                pltpu.VMEM((2, 8, DIM), f32),
                pltpu.VMEM((3, 8, DIM), f32),
                pltpu.VMEM((3, most, 8, DIM), f32),
                pltpu.SemaphoreType.DMA((2 * HEADS + 2,)),
            ]
            + [pltpu.SemaphoreType.DMA((HEADS, 2)) for _ in range(4)]
            + [pltpu.SemaphoreType.DMA((HEADS, 2, 2)) for _ in range(4)]
            + [pltpu.SemaphoreType.DMA((3, most)) for _ in range(2)],
            compiler_params=pltpu.CompilerParams(
                collective_id=0, has_side_effects=True, vmem_limit_bytes=58 * 1024 * 1024
            ),
        )(
            q,
            k,
            v,
            out_grad,
            query_gain[None],
            key_gain[None],
            inverse_freq,
            doc_starts,
            windows,
        )
        dq, dk, dv, dq_gain, dk_gain = pl.pallas_call(
            write_out,
            out_shape=tuple(jax.ShapeDtypeStruct(x.shape, x.dtype) for x in results),
            in_specs=[pl.BlockSpec(memory_space=pl.ANY)] * 5,
            out_specs=(pl.BlockSpec(memory_space=pl.ANY),) * 5,
            scratch_shapes=[pltpu.SemaphoreType.DMA((5,))],
            compiler_params=pltpu.CompilerParams(vmem_limit_bytes=4 * 1024 * 1024),
        )(*results)
        return dq, dk, dv, dq_gain[0], dk_gain[0]

    split = P("seq", "head")
    return jax.shard_map(
        step,
        mesh=mesh,
        in_specs=(split,) * 4 + (P(),) * 4,
        out_specs=(split, split, split, P(), P()),
        check_vma=False,
    )
```

```python
import functools
import math

import jax
import jax.numpy as jnp
import numpy as np
from jax import lax
from jax.experimental import pallas as pl
from jax.experimental.pallas import tpu as pltpu
from jax.sharding import PartitionSpec as P

SLABS = 4
ROWS = 512
TILE = 256
SPAN = 1280
KEYS = 1536
DIM = 128
HEADS = 4

score_scale = 168.0 ** (-0.5)
exp2_scale = score_scale * math.log2(math.e)
norm_eps = 1e-06
masked_score = -1e30
f32 = jnp.float32
bf16 = jnp.bfloat16
MESH = pl.DeviceIdType.MESH


def half_turn(x):
    return pltpu.roll(x, DIM // 2, 1)


def unit_rows(raw):
    x = raw.astype(f32)
    inverse = lax.rsqrt(jnp.mean(x * x, axis=-1, keepdims=True) + norm_eps)
    return x * inverse, inverse


def fold_rows(x):
    return jnp.sum(x.reshape(x.shape[0] // 8, 8, DIM), axis=0)


def cos_sin(angle, cos_lane):
    turns = jnp.floor(angle * (2.0 / math.pi) + 0.5)
    rest = angle - turns * 1.5703125
    rest = rest - turns * 4.837512969970703e-4
    rest = rest - turns * 7.549789954891882e-8
    square = rest * rest
    sine = rest + rest * square * (
        -1.6666654611e-1 + square * (8.3321608736e-3 - square * 1.9515295891e-4)
    )
    cosine = 1.0 - 0.5 * square + square * square * (
        4.166664568298827e-2 + square * (-1.388731625493765e-3 + square * 2.443315711809948e-5)
    )
    quarter = turns + jnp.where(cos_lane, 1.0, 0.0)
    quarter = quarter - 4.0 * jnp.floor(quarter * 0.25)
    odd = (quarter == 1.0) | (quarter == 3.0)
    value = jnp.where(odd, cosine, sine)
    return jnp.where(quarter >= 2.0, -value, value)


def kernel(
    shards,
    heads,
    q_hbm,
    k_hbm,
    v_hbm,
    do_hbm,
    query_gain,
    key_gain,
    inverse_freq,
    doc_starts,
    windows,
    dq_all,
    dk_all,
    dv_all,
    query_gain_out,
    key_gain_out,
    kcat,
    vcat,
    q_all,
    do_all,
    cos_table,
    sin_table,
    khat,
    kunit,
    qhat,
    qunit,
    qinv,
    dos,
    scores,
    soft_grad,
    acc_k,
    acc_v,
    far_send,
    far_in,
    near_send,
    near_in,
    gain_acc,
    sum_send,
    sum_in,
    local_sem,
    fwd_send,
    fwd_recv,
    relay_send,
    relay_recv,
    far_ssem,
    far_rsem,
    near_ssem,
    near_rsem,
    sum_ssem,
    sum_rsem,
):
    total = shards * ROWS
    length = total // SLABS
    me = lax.axis_index("seq")
    my_head = lax.axis_index("head")
    ahead = lax.rem(me + 1, shards)
    behind = lax.rem(me + shards - 1, shards)
    low_size = min(8, shards)
    high_size = shards // low_size
    my_low = lax.rem(me, low_size)
    my_high = me // low_size
    stages = [
        (low_size, my_low, lambda n: (my_high * low_size + n, my_head)),
        (heads, my_head, lambda n: (me, n)),
        (high_size, my_high, lambda n: (n * low_size + my_low, my_head)),
    ]

    barrier = pltpu.get_barrier_semaphore()
    pl.semaphore_signal(barrier, inc=1, device_id=(ahead, my_head), device_id_type=MESH)
    pl.semaphore_signal(barrier, inc=1, device_id=(behind, my_head), device_id_type=MESH)
    greeted = 2
    for size, mine, place in stages:
        for k in range(1, size):
            pl.semaphore_signal(
                barrier,
                inc=1,
                device_id=place(lax.rem(mine + k, size)),
                device_id_type=MESH,
            )
            greeted += 1
    pl.semaphore_wait(barrier, greeted)

    def columns(j, width=DIM):
        return pl.ds(pl.multiple_of(j * width, width), width)

    def own_copies(j, which=(0, 1)):
        return [
            pltpu.make_async_remote_copy(
                src_ref=src.at[:, columns(j)],
                dst_ref=dst.at[j, pl.ds(ROWS, ROWS), :],
                send_sem=fwd_send.at[j, n],
                recv_sem=fwd_recv.at[j, n],
                device_id=(ahead, my_head),
                device_id_type=MESH,
            )
            for n, (src, dst) in enumerate(((k_hbm, kcat), (v_hbm, vcat)))
            if n in which
        ]

    def relay_copies(j, which=(0, 1)):
        return [
            pltpu.make_async_remote_copy(
                src_ref=buf.at[j, pl.ds(ROWS, ROWS), :],
                dst_ref=buf.at[j, pl.ds(0, ROWS), :],
                send_sem=relay_send.at[j, n],
                recv_sem=relay_recv.at[j, n],
                device_id=(ahead, my_head),
                device_id_type=MESH,
            )
            for n, buf in enumerate((kcat, vcat))
            if n in which
        ]

    def back_copies(j, half, which, src, dst, ssem, rsem):
        rows = pl.ds(pl.multiple_of(half * TILE, TILE), TILE)
        return [
            pltpu.make_async_remote_copy(
                src_ref=src.at[j, n, rows, :],
                dst_ref=dst.at[j, n, rows, :],
                send_sem=ssem.at[j, n, half],
                recv_sem=rsem.at[j, n, half],
                device_id=(behind, my_head),
                device_id_type=MESH,
            )
            for n in which
        ]

    def far_copies(j, half, which=(0, 1)):
        return back_copies(j, half, which, far_send, far_in, far_ssem, far_rsem)

    def near_copies(j, half, which=(0, 1)):
        return back_copies(j, half, which, near_send, near_in, near_ssem, near_rsem)

    def start_own(j, n):
        own_copies(j, (n,))[0].start()

    def relay(j, n):
        own_copies(j, (n,))[0].wait_recv()
        relay_copies(j, (n,))[0].start()

    start_own(0, 0)
    start_own(0, 1)
    start_own(1, 0)
    local = []
    for j in range(HEADS):
        local.append((k_hbm.at[:, columns(j)], kcat.at[j, pl.ds(2 * ROWS, ROWS), :]))
        local.append((v_hbm.at[:, columns(j)], vcat.at[j, pl.ds(2 * ROWS, ROWS), :]))
    local.append((q_hbm, q_all))
    local.append((do_hbm, do_all))
    local = [
        pltpu.make_async_copy(src, dst, local_sem.at[n]) for n, (src, dst) in enumerate(local)
    ]
    for copy in local:
        copy.start()

    def block_info(block):
        shard = lax.rem(me + shards - 2 + block, shards)
        placed = lax.rem(shard * ROWS + total - length // 2, total)
        slab = placed // length
        return slab, placed - slab * length

    def rope_position(in_slab, slab):
        begin = jnp.zeros_like(in_slab)
        for n in range(doc_starts.shape[1]):
            start = doc_starts[slab, n]
            begin = jnp.where(in_slab >= start, jnp.maximum(begin, start), begin)
        return in_slab - begin

    lane = lax.broadcasted_iota(jnp.int32, (TILE, DIM), 1)
    cos_lane = lane < DIM // 2

    def table_step(n, carry):
        block = n // (ROWS // TILE)
        slab, first = block_info(block)
        offset = lax.rem(n, ROWS // TILE) * TILE
        in_slab = first + offset + lax.broadcasted_iota(jnp.int32, (TILE, DIM), 0)
        position = rope_position(in_slab, slab).astype(f32)
        both = cos_sin(position * inverse_freq[...], cos_lane)
        other = half_turn(both)
        here = pl.ds(pl.multiple_of(n * TILE, TILE), TILE)
        cos_table[here, :] = jnp.where(cos_lane, both, other)
        sin_table[here, :] = jnp.where(cos_lane, -other, both)
        return carry

    lax.fori_loop(0, KEYS // TILE, table_step, 0)
    gain_acc[...] = jnp.zeros_like(gain_acc)

    for copy in local:
        copy.wait()
    relay(0, 0)
    relay(0, 1)
    start_own(1, 1)
    start_own(2, 0)
    relay(1, 0)

    slab, first = block_info(2)
    window = windows[slab]

    def key_norm(j, start, count):
        def step(n, carry):
            here = pl.ds(pl.multiple_of(start + n * TILE, TILE), TILE)
            unit, _ = unit_rows(kcat[j, here, :])
            scaled = unit * key_gain[...]
            khat[here, :] = (
                scaled * cos_table[here, :] + half_turn(scaled) * sin_table[here, :]
            ).astype(bf16)
            kunit[here, :] = unit
            return carry

        lax.fori_loop(0, count // TILE, step, 0)

    nt = (((1,), (1,)), ((), ()))
    nn = (((1,), (0,)), ((), ()))
    tn = (((0,), (0,)), ((), ()))

    def attend(j, i):
        base = i * TILE
        rows = pl.ds(pl.multiple_of(base, TILE), TILE)
        mine = pl.ds(pl.multiple_of(base + 2 * ROWS, TILE), TILE)
        for g in range(2):
            head_columns = pl.ds(pl.multiple_of((2 * j + g) * DIM, DIM), DIM)
            part = pl.ds(g * TILE, TILE)
            unit, inverse = unit_rows(q_all[rows, head_columns])
            scaled = unit * query_gain[...]
            qhat[part, :] = (
                scaled * cos_table[mine, :] + half_turn(scaled) * sin_table[mine, :]
            ).astype(bf16)
            qunit[part, :] = unit
            qinv[part, :] = jnp.broadcast_to(inverse, (TILE, DIM))
            dos[part, :] = do_all[rows, head_columns]
        row = lax.broadcasted_iota(jnp.int32, (1, TILE), 1)
        in_slab = first + base + row
        reach = jnp.minimum(rope_position(in_slab, slab), window - 1)
        lowest = 2 * ROWS + row - reach
        key_row = lax.broadcasted_iota(jnp.int32, (TILE, TILE), 0)
        q = [qhat[pl.ds(g * TILE, TILE), :] for g in range(2)]
        out_grad = [dos[pl.ds(g * TILE, TILE), :] for g in range(2)]
        row_max = [jnp.full((1, TILE), masked_score, f32)] * 2
        row_sum = [jnp.zeros((1, TILE), f32)] * 2
        delta = [jnp.zeros((1, TILE), f32)] * 2
        query_grad = [jnp.zeros((DIM, TILE), f32)] * 2
        tiles = SPAN // TILE

        def there(t):
            return pl.ds(pl.multiple_of(base + t * TILE, TILE), TILE)

        def here(t):
            return pl.ds(t * TILE, TILE)

        def score_tile(g, t):
            tile = lax.dot_general(khat[there(t), :], q[g], nt, preferred_element_type=f32)
            visible = key_row >= lowest - t * TILE
            if t == tiles - 1:
                visible = visible & (key_row <= row)
            tile = jnp.where(visible, tile, masked_score)
            scores[g, here(t), :] = tile
            row_max[g] = jnp.maximum(row_max[g], jnp.max(tile, axis=0, keepdims=True))

        def gradient_tile(g, t):
            soft_grad[g, here(t), :] = lax.dot_general(
                vcat[j, there(t), :], out_grad[g], nt, preferred_element_type=f32
            )

        def exponent_tile(g, t):
            exponent = jnp.exp2(scores[g, here(t), :] * exp2_scale - row_max[g])
            row_sum[g] = row_sum[g] + jnp.sum(exponent, axis=0, keepdims=True)
            delta[g] = delta[g] + jnp.sum(
                exponent * soft_grad[g, here(t), :], axis=0, keepdims=True
            )
            scores[g, here(t), :] = exponent

        def product_tile(g, t):
            softmax = scores[g, here(t), :] * row_sum[g]
            grad_scores = (softmax * (soft_grad[g, here(t), :] - delta[g])).astype(bf16)
            acc_v[j, there(t), :] += lax.dot_general(
                softmax.astype(bf16), out_grad[g], nn, preferred_element_type=f32
            )
            acc_k[j, there(t), :] += lax.dot_general(
                grad_scores, q[g], nn, preferred_element_type=f32
            )
            query_grad[g] = query_grad[g] + lax.dot_general(
                khat[there(t), :], grad_scores, tn, preferred_element_type=f32
            )

        def close_max(g):
            row_max[g] = row_max[g] * exp2_scale

        def close_sum(g):
            row_sum[g] = 1.0 / row_sum[g]
            delta[g] = delta[g] * row_sum[g]

        for g in range(2):
            for t in range(tiles):
                score_tile(g, t)
            close_max(g)

        @pl.when(i == 0)
        def _():
            relay_copies(j, (1,))[0].wait_recv()

        for t in range(tiles):
            gradient_tile(0, t)
        for t in range(tiles):
            exponent_tile(0, t)
        close_sum(0)
        for t in range(tiles):
            gradient_tile(1, t)
            product_tile(0, t)
            exponent_tile(1, t)
        close_sum(1)
        for t in range(tiles):
            product_tile(1, t)
        for g in range(2):
            head_columns = pl.ds(pl.multiple_of((2 * j + g) * DIM, DIM), DIM)
            part = pl.ds(g * TILE, TILE)
            grad = query_grad[g].T * score_scale
            turned = grad * cos_table[mine, :] - half_turn(grad) * sin_table[mine, :]
            unit = qunit[part, :]
            gain_acc[0] += fold_rows(turned * unit)
            weighted = turned * query_gain[...]
            mean = jnp.mean(weighted * unit, axis=-1, keepdims=True)
            dq_all[rows, head_columns] = (qinv[part, :] * (weighted - unit * mean)).astype(bf16)

    def hand_on(j, half, which=(0, 1)):
        rows = pl.ds(half * TILE, TILE)
        for n in which:
            acc = (acc_k, acc_v)[n]
            far_copies(j, half, (n,))[0].wait_recv()
            near_send[j, n, rows, :] = (
                far_in[j, n, rows, :].astype(f32) + acc[j, pl.ds(ROWS + half * TILE, TILE), :]
            ).astype(bf16)
            near_copies(j, half, (n,))[0].start()

    def finish(j, half):
        rows = pl.ds(half * TILE, TILE)
        mine = pl.ds(2 * ROWS + half * TILE, TILE)
        unit, inverse = unit_rows(kcat[j, mine, :])
        near_copies(j, half, (0,))[0].wait_recv()
        grad = (near_in[j, 0, rows, :].astype(f32) + acc_k[j, mine, :]) * score_scale
        turned = grad * cos_table[mine, :] - half_turn(grad) * sin_table[mine, :]
        weighted = turned * key_gain[...]
        mean = jnp.mean(weighted * unit, axis=-1, keepdims=True)
        dk_all[rows, columns(j)] = (inverse * (weighted - unit * mean)).astype(bf16)
        near_copies(j, half, (1,))[0].wait_recv()
        dv_all[rows, columns(j)] = (
            near_in[j, 1, rows, :].astype(f32) + acc_v[j, mine, :]
        ).astype(bf16)

    def between(j):
        @pl.when(j < 3)
        def _():
            relay(j + 1, 1)

        @pl.when(j < 2)
        def _():
            start_own(j + 2, 1)

        @pl.when(j == 0)
        def _():
            start_own(3, 0)

        @pl.when(j >= 1)
        def _():
            hand_on(j - 1, 1, (0,))

        @pl.when((j >= 1) & (j < 3))
        def _():
            hand_on(j - 1, 1, (1,))

        @pl.when(j == 2)
        def _():
            finish(0, 0)
            finish(0, 1)

    def sum_copy(n, k):
        size, mine, place = stages[n]
        return pltpu.make_async_remote_copy(
            src_ref=sum_send.at[n],
            dst_ref=sum_in.at[n, mine],
            send_sem=sum_ssem.at[n, k],
            recv_sem=sum_rsem.at[n, mine],
            device_id=place(lax.rem(mine + k, size)),
            device_id_type=MESH,
        )

    def sum_arrival(n, k):
        size, mine, place = stages[n]
        source = lax.rem(mine + size - k, size)
        return pltpu.make_async_remote_copy(
            src_ref=sum_send.at[n],
            dst_ref=sum_in.at[n, source],
            send_sem=sum_ssem.at[n, k],
            recv_sem=sum_rsem.at[n, source],
            device_id=place(source),
            device_id_type=MESH,
        )

    def start_sum(n, value):
        size, mine, place = stages[n]
        sum_send[n] = value
        sum_in[n, mine] = value
        for k in range(1, size):
            sum_copy(n, k).start()

    def end_sum(n):
        size, mine, place = stages[n]
        for k in range(1, size):
            sum_arrival(n, k).wait_recv()
        value = sum_in[n, 0]
        for k in range(1, size):
            value = value + sum_in[n, k]
        return value

    def gain_part(j):
        def gain_step(n, inner):
            here = pl.ds(pl.multiple_of(n * TILE, TILE), TILE)
            grad = acc_k[j, here, :] * score_scale
            turned = grad * cos_table[here, :] - half_turn(grad) * sin_table[here, :]
            gain_acc[1] += fold_rows(turned * kunit[here, :])
            return inner

        lax.fori_loop(0, KEYS // TILE, gain_step, 0)

    def last_gain(j):
        gain_part(j)
        spread = jnp.where(
            lax.broadcasted_iota(jnp.int32, (8, DIM), 0) == 0,
            jnp.sum(gain_acc[0], axis=0, keepdims=True),
            jnp.sum(gain_acc[1], axis=0, keepdims=True),
        )
        start_sum(0, spread)

    def head_step(j, carry):
        @pl.when(j >= 1)
        def _():
            hand_on(j - 1, 0)

        key_norm(j, ROWS, 2 * ROWS)
        acc_k[j] = jnp.zeros((KEYS, DIM), f32)
        acc_v[j] = jnp.zeros((KEYS, DIM), f32)
        relay_copies(j, (0,))[0].wait_recv()
        key_norm(j, 0, ROWS)

        def row_step(i, inner):
            attend(j, i)

            @pl.when(2 * j + i == 2 * HEADS - 1)
            def _():
                last_gain(j)

            rows = pl.ds(pl.multiple_of(i * TILE, TILE), TILE)
            far_send[j, 0, rows, :] = acc_k[j, rows, :].astype(bf16)
            far_send[j, 1, rows, :] = acc_v[j, rows, :].astype(bf16)
            for copy in far_copies(j, i):
                copy.start()

            @pl.when(i == 0)
            def _():
                between(j)

            return inner

        lax.fori_loop(0, ROWS // TILE, row_step, 0)

        @pl.when(j < 2)
        def _():
            relay(j + 2, 0)

        @pl.when(j < 3)
        def _():
            gain_part(j)

        return carry

    lax.fori_loop(0, HEADS, head_step, 0)

    hand_on(2, 1, (1,))
    hand_on(3, 0)
    finish(1, 0)
    finish(1, 1)
    hand_on(3, 1, (0,))
    start_sum(1, end_sum(0))
    hand_on(3, 1, (1,))
    start_sum(2, end_sum(1))
    finish(2, 0)
    finish(2, 1)
    finish(3, 0)
    gains = end_sum(2)
    query_gain_out[...] = gains[0:1]
    key_gain_out[...] = gains[1:2]
    finish(3, 1)

    for n, (size, mine, place) in enumerate(stages):
        for k in range(1, size):
            sum_copy(n, k).wait_send()

    def drain(j, carry):
        backward = [copy(j, half) for copy in (far_copies, near_copies) for half in range(2)]
        for copies in (own_copies(j), relay_copies(j), *backward):
            for copy in copies:
                copy.wait_send()
        return carry

    lax.fori_loop(0, HEADS, drain, 0)


def write_out(*refs):
    sources, targets, sem = refs[:5], refs[5:10], refs[10]
    copies = [
        pltpu.make_async_copy(src, dst, sem.at[n])
        for n, (src, dst) in enumerate(zip(sources, targets))
    ]
    for copy in copies:
        copy.start()
    for copy in copies:
        copy.wait()


def solution(mesh):
    shards, heads = mesh.shape["seq"], mesh.shape["head"]
    most = max(heads, 8, shards // 8)

    def step(q, k, v, out_grad, query_gain, key_gain, doc_starts, windows):
        inverse_freq = 10000.0 ** (-np.arange(DIM // 2, dtype=np.float64) * (2.0 / DIM))
        inverse_freq = jnp.asarray(np.tile(inverse_freq, 2)[None], f32)
        hbm = pl.BlockSpec(memory_space=pltpu.HBM)
        vmem = pl.BlockSpec(memory_space=pltpu.VMEM)
        smem = pl.BlockSpec(memory_space=pltpu.SMEM)
        results = pl.pallas_call(
            functools.partial(kernel, shards, heads),
            out_shape=(
                pltpu.VMEM(q.shape, bf16),
                pltpu.VMEM(k.shape, bf16),
                pltpu.VMEM(v.shape, bf16),
                pltpu.VMEM((1, DIM), f32),
                pltpu.VMEM((1, DIM), f32),
            ),
            in_specs=[hbm] * 4 + [vmem] * 3 + [smem] * 2,
            out_specs=(vmem,) * 5,
            scratch_shapes=[
                pltpu.VMEM((HEADS, KEYS, DIM), bf16),
                pltpu.VMEM((HEADS, KEYS, DIM), bf16),
                pltpu.VMEM((ROWS, 2 * HEADS * DIM), bf16),
                pltpu.VMEM((ROWS, 2 * HEADS * DIM), bf16),
                pltpu.VMEM((KEYS, DIM), f32),
                pltpu.VMEM((KEYS, DIM), f32),
                pltpu.VMEM((KEYS, DIM), bf16),
                pltpu.VMEM((KEYS, DIM), f32),
                pltpu.VMEM((2 * TILE, DIM), bf16),
                pltpu.VMEM((2 * TILE, DIM), f32),
                pltpu.VMEM((2 * TILE, DIM), f32),
                pltpu.VMEM((2 * TILE, DIM), bf16),
                pltpu.VMEM((2, SPAN, TILE), f32),
                pltpu.VMEM((2, SPAN, TILE), f32),
                pltpu.VMEM((HEADS, KEYS, DIM), f32),
                pltpu.VMEM((HEADS, KEYS, DIM), f32),
                pltpu.VMEM((HEADS, 2, ROWS, DIM), bf16),
                pltpu.VMEM((HEADS, 2, ROWS, DIM), bf16),
                pltpu.VMEM((HEADS, 2, ROWS, DIM), bf16),
                pltpu.VMEM((HEADS, 2, ROWS, DIM), bf16),
                pltpu.VMEM((2, 8, DIM), f32),
                pltpu.VMEM((3, 8, DIM), f32),
                pltpu.VMEM((3, most, 8, DIM), f32),
                pltpu.SemaphoreType.DMA((2 * HEADS + 2,)),
            ]
            + [pltpu.SemaphoreType.DMA((HEADS, 2)) for _ in range(4)]
            + [pltpu.SemaphoreType.DMA((HEADS, 2, 2)) for _ in range(4)]
            + [pltpu.SemaphoreType.DMA((3, most)) for _ in range(2)],
            compiler_params=pltpu.CompilerParams(
                collective_id=0, has_side_effects=True, vmem_limit_bytes=58 * 1024 * 1024
            ),
        )(
            q,
            k,
            v,
            out_grad,
            query_gain[None],
            key_gain[None],
            inverse_freq,
            doc_starts,
            windows,
        )
        dq, dk, dv, dq_gain, dk_gain = pl.pallas_call(
            write_out,
            out_shape=tuple(jax.ShapeDtypeStruct(x.shape, x.dtype) for x in results),
            in_specs=[pl.BlockSpec(memory_space=pl.ANY)] * 5,
            out_specs=(pl.BlockSpec(memory_space=pl.ANY),) * 5,
            scratch_shapes=[pltpu.SemaphoreType.DMA((5,))],
            compiler_params=pltpu.CompilerParams(vmem_limit_bytes=4 * 1024 * 1024),
        )(*results)
        return dq, dk, dv, dq_gain[0], dk_gain[0]

    split = P("seq", "head")
    return jax.shard_map(
        step,
        mesh=mesh,
        in_specs=(split,) * 4 + (P(),) * 4,
        out_specs=(split, split, split, P(), P()),
        check_vma=False,
    )
```

```python
import functools
import math

import jax
import jax.numpy as jnp
import numpy as np
from jax import lax
from jax.experimental import pallas as pl
from jax.experimental.pallas import tpu as pltpu
from jax.sharding import PartitionSpec as P

SLABS = 4
ROWS = 512
TILE = 256
SPAN = 1280
KEYS = 1536
DIM = 128
HEADS = 4

score_scale = 168.0 ** (-0.5)
exp2_scale = score_scale * math.log2(math.e)
norm_eps = 1e-06
masked_score = -1e30
f32 = jnp.float32
bf16 = jnp.bfloat16
MESH = pl.DeviceIdType.MESH


def half_turn(x):
    return pltpu.roll(x, DIM // 2, 1)


def unit_rows(raw):
    x = raw.astype(f32)
    inverse = lax.rsqrt(jnp.mean(x * x, axis=-1, keepdims=True) + norm_eps)
    return x * inverse, inverse


def fold_rows(x):
    return jnp.sum(x.reshape(x.shape[0] // 8, 8, DIM), axis=0)


def cos_sin(angle, cos_lane):
    turns = jnp.floor(angle * (2.0 / math.pi) + 0.5)
    rest = angle - turns * 1.5703125
    rest = rest - turns * 4.837512969970703e-4
    rest = rest - turns * 7.549789954891882e-8
    square = rest * rest
    sine = rest + rest * square * (
        -1.6666654611e-1 + square * (8.3321608736e-3 - square * 1.9515295891e-4)
    )
    cosine = 1.0 - 0.5 * square + square * square * (
        4.166664568298827e-2 + square * (-1.388731625493765e-3 + square * 2.443315711809948e-5)
    )
    quarter = turns + jnp.where(cos_lane, 1.0, 0.0)
    quarter = quarter - 4.0 * jnp.floor(quarter * 0.25)
    odd = (quarter == 1.0) | (quarter == 3.0)
    value = jnp.where(odd, cosine, sine)
    return jnp.where(quarter >= 2.0, -value, value)


def kernel(
    shards,
    heads,
    q_hbm,
    k_hbm,
    v_hbm,
    do_hbm,
    query_gain,
    key_gain,
    inverse_freq,
    doc_starts,
    windows,
    dq_all,
    dk_all,
    dv_all,
    query_gain_out,
    key_gain_out,
    kcat,
    vcat,
    q_all,
    do_all,
    cos_table,
    sin_table,
    khat,
    kunit,
    qhat,
    qunit,
    qinv,
    dos,
    scores,
    soft_grad,
    acc_k,
    acc_v,
    far_send,
    far_in,
    near_send,
    near_in,
    gain_acc,
    sum_send,
    sum_in,
    local_sem,
    fwd_send,
    fwd_recv,
    relay_send,
    relay_recv,
    far_ssem,
    far_rsem,
    near_ssem,
    near_rsem,
    sum_ssem,
    sum_rsem,
):
    total = shards * ROWS
    length = total // SLABS
    me = lax.axis_index("seq")
    my_head = lax.axis_index("head")
    ahead = lax.rem(me + 1, shards)
    behind = lax.rem(me + shards - 1, shards)
    low_size = min(8, shards)
    high_size = shards // low_size
    my_low = lax.rem(me, low_size)
    my_high = me // low_size
    stages = [
        (low_size, my_low, lambda n: (my_high * low_size + n, my_head)),
        (heads, my_head, lambda n: (me, n)),
        (high_size, my_high, lambda n: (n * low_size + my_low, my_head)),
    ]

    barrier = pltpu.get_barrier_semaphore()
    pl.semaphore_signal(barrier, inc=1, device_id=(ahead, my_head), device_id_type=MESH)
    pl.semaphore_signal(barrier, inc=1, device_id=(behind, my_head), device_id_type=MESH)
    greeted = 2
    for size, mine, place in stages:
        for k in range(1, size):
            pl.semaphore_signal(
                barrier,
                inc=1,
                device_id=place(lax.rem(mine + k, size)),
                device_id_type=MESH,
            )
            greeted += 1
    pl.semaphore_wait(barrier, greeted)

    def columns(j, width=DIM):
        return pl.ds(pl.multiple_of(j * width, width), width)

    def own_copies(j, which=(0, 1)):
        return [
            pltpu.make_async_remote_copy(
                src_ref=src.at[:, columns(j)],
                dst_ref=dst.at[j, pl.ds(ROWS, ROWS), :],
                send_sem=fwd_send.at[j, n],
                recv_sem=fwd_recv.at[j, n],
                device_id=(ahead, my_head),
                device_id_type=MESH,
            )
            for n, (src, dst) in enumerate(((k_hbm, kcat), (v_hbm, vcat)))
            if n in which
        ]

    def relay_copies(j, which=(0, 1)):
        return [
            pltpu.make_async_remote_copy(
                src_ref=buf.at[j, pl.ds(ROWS, ROWS), :],
                dst_ref=buf.at[j, pl.ds(0, ROWS), :],
                send_sem=relay_send.at[j, n],
                recv_sem=relay_recv.at[j, n],
                device_id=(ahead, my_head),
                device_id_type=MESH,
            )
            for n, buf in enumerate((kcat, vcat))
            if n in which
        ]

    def back_copies(j, half, which, src, dst, ssem, rsem):
        rows = pl.ds(pl.multiple_of(half * TILE, TILE), TILE)
        return [
            pltpu.make_async_remote_copy(
                src_ref=src.at[j, n, rows, :],
                dst_ref=dst.at[j, n, rows, :],
                send_sem=ssem.at[j, n, half],
                recv_sem=rsem.at[j, n, half],
                device_id=(behind, my_head),
                device_id_type=MESH,
            )
            for n in which
        ]

    def far_copies(j, half, which=(0, 1)):
        return back_copies(j, half, which, far_send, far_in, far_ssem, far_rsem)

    def near_copies(j, half, which=(0, 1)):
        return back_copies(j, half, which, near_send, near_in, near_ssem, near_rsem)

    def start_own(j, n):
        own_copies(j, (n,))[0].start()

    def relay(j, n):
        own_copies(j, (n,))[0].wait_recv()
        relay_copies(j, (n,))[0].start()

    start_own(0, 0)
    start_own(0, 1)
    start_own(1, 0)
    local = []
    for j in range(HEADS):
        local.append((k_hbm.at[:, columns(j)], kcat.at[j, pl.ds(2 * ROWS, ROWS), :]))
        local.append((v_hbm.at[:, columns(j)], vcat.at[j, pl.ds(2 * ROWS, ROWS), :]))
    local.append((q_hbm, q_all))
    local.append((do_hbm, do_all))
    local = [
        pltpu.make_async_copy(src, dst, local_sem.at[n]) for n, (src, dst) in enumerate(local)
    ]
    for copy in local:
        copy.start()

    def block_info(block):
        shard = lax.rem(me + shards - 2 + block, shards)
        placed = lax.rem(shard * ROWS + total - length // 2, total)
        slab = placed // length
        return slab, placed - slab * length

    def rope_position(in_slab, slab):
        begin = jnp.zeros_like(in_slab)
        for n in range(doc_starts.shape[1]):
            start = doc_starts[slab, n]
            begin = jnp.where(in_slab >= start, jnp.maximum(begin, start), begin)
        return in_slab - begin

    lane = lax.broadcasted_iota(jnp.int32, (TILE, DIM), 1)
    cos_lane = lane < DIM // 2

    def table_step(n, carry):
        block = n // (ROWS // TILE)
        slab, first = block_info(block)
        offset = lax.rem(n, ROWS // TILE) * TILE
        in_slab = first + offset + lax.broadcasted_iota(jnp.int32, (TILE, DIM), 0)
        position = rope_position(in_slab, slab).astype(f32)
        both = cos_sin(position * inverse_freq[...], cos_lane)
        other = half_turn(both)
        here = pl.ds(pl.multiple_of(n * TILE, TILE), TILE)
        cos_table[here, :] = jnp.where(cos_lane, both, other)
        sin_table[here, :] = jnp.where(cos_lane, -other, both)
        return carry

    lax.fori_loop(0, KEYS // TILE, table_step, 0)
    gain_acc[...] = jnp.zeros_like(gain_acc)

    for copy in local:
        copy.wait()
    relay(0, 0)
    relay(0, 1)
    start_own(1, 1)
    start_own(2, 0)
    relay(1, 0)

    slab, first = block_info(2)
    window = windows[slab]

    def key_norm(j, start, count):
        def step(n, carry):
            here = pl.ds(pl.multiple_of(start + n * TILE, TILE), TILE)
            unit, _ = unit_rows(kcat[j, here, :])
            scaled = unit * key_gain[...]
            khat[here, :] = (
                scaled * cos_table[here, :] + half_turn(scaled) * sin_table[here, :]
            ).astype(bf16)
            kunit[here, :] = unit
            return carry

        lax.fori_loop(0, count // TILE, step, 0)

    nt = (((1,), (1,)), ((), ()))
    nn = (((1,), (0,)), ((), ()))
    tn = (((0,), (0,)), ((), ()))

    def attend(j, i):
        base = i * TILE
        rows = pl.ds(pl.multiple_of(base, TILE), TILE)
        mine = pl.ds(pl.multiple_of(base + 2 * ROWS, TILE), TILE)
        for g in range(2):
            head_columns = pl.ds(pl.multiple_of((2 * j + g) * DIM, DIM), DIM)
            part = pl.ds(g * TILE, TILE)
            unit, inverse = unit_rows(q_all[rows, head_columns])
            scaled = unit * query_gain[...]
            qhat[part, :] = (
                scaled * cos_table[mine, :] + half_turn(scaled) * sin_table[mine, :]
            ).astype(bf16)
            qunit[part, :] = unit
            qinv[part, :] = jnp.broadcast_to(inverse, (TILE, DIM))
            dos[part, :] = do_all[rows, head_columns]
        row = lax.broadcasted_iota(jnp.int32, (1, TILE), 1)
        in_slab = first + base + row
        reach = jnp.minimum(rope_position(in_slab, slab), window - 1)
        lowest = 2 * ROWS + row - reach
        key_row = lax.broadcasted_iota(jnp.int32, (TILE, TILE), 0)
        q = [qhat[pl.ds(g * TILE, TILE), :] for g in range(2)]
        out_grad = [dos[pl.ds(g * TILE, TILE), :] for g in range(2)]
        row_max = [jnp.full((1, TILE), masked_score, f32)] * 2
        row_sum = [jnp.zeros((1, TILE), f32)] * 2
        delta = [jnp.zeros((1, TILE), f32)] * 2
        query_grad = [jnp.zeros((DIM, TILE), f32)] * 2
        tiles = SPAN // TILE

        def there(t):
            return pl.ds(pl.multiple_of(base + t * TILE, TILE), TILE)

        def here(t):
            return pl.ds(t * TILE, TILE)

        def score_tile(g, t):
            tile = lax.dot_general(khat[there(t), :], q[g], nt, preferred_element_type=f32)
            visible = key_row >= lowest - t * TILE
            if t == tiles - 1:
                visible = visible & (key_row <= row)
            tile = jnp.where(visible, tile, masked_score)
            scores[g, here(t), :] = tile
            row_max[g] = jnp.maximum(row_max[g], jnp.max(tile, axis=0, keepdims=True))

        def gradient_tile(g, t):
            soft_grad[g, here(t), :] = lax.dot_general(
                vcat[j, there(t), :], out_grad[g], nt, preferred_element_type=f32
            )

        def exponent_tile(g, t):
            exponent = jnp.exp2(scores[g, here(t), :] * exp2_scale - row_max[g])
            row_sum[g] = row_sum[g] + jnp.sum(exponent, axis=0, keepdims=True)
            delta[g] = delta[g] + jnp.sum(
                exponent * soft_grad[g, here(t), :], axis=0, keepdims=True
            )
            scores[g, here(t), :] = exponent

        def product_tile(g, t):
            softmax = scores[g, here(t), :] * row_sum[g]
            grad_scores = (softmax * (soft_grad[g, here(t), :] - delta[g])).astype(bf16)
            acc_v[j, there(t), :] += lax.dot_general(
                softmax.astype(bf16), out_grad[g], nn, preferred_element_type=f32
            )
            acc_k[j, there(t), :] += lax.dot_general(
                grad_scores, q[g], nn, preferred_element_type=f32
            )
            query_grad[g] = query_grad[g] + lax.dot_general(
                khat[there(t), :], grad_scores, tn, preferred_element_type=f32
            )

        def close_max(g):
            row_max[g] = row_max[g] * exp2_scale

        def close_sum(g):
            row_sum[g] = 1.0 / row_sum[g]
            delta[g] = delta[g] * row_sum[g]

        for g in range(2):
            for t in range(tiles):
                score_tile(g, t)
            close_max(g)

        @pl.when(i == 0)
        def _():
            relay_copies(j, (1,))[0].wait_recv()

        for g in range(2):
            for t in range(tiles):
                gradient_tile(g, t)
        for t in range(tiles):
            exponent_tile(0, t)
        close_sum(0)
        for t in range(tiles):
            product_tile(0, t)
            exponent_tile(1, t)
        close_sum(1)
        for t in range(tiles):
            product_tile(1, t)
        for g in range(2):
            head_columns = pl.ds(pl.multiple_of((2 * j + g) * DIM, DIM), DIM)
            part = pl.ds(g * TILE, TILE)
            grad = query_grad[g].T * score_scale
            turned = grad * cos_table[mine, :] - half_turn(grad) * sin_table[mine, :]
            unit = qunit[part, :]
            gain_acc[0] += fold_rows(turned * unit)
            weighted = turned * query_gain[...]
            mean = jnp.mean(weighted * unit, axis=-1, keepdims=True)
            dq_all[rows, head_columns] = (qinv[part, :] * (weighted - unit * mean)).astype(bf16)

    def hand_on(j, half, which=(0, 1)):
        rows = pl.ds(half * TILE, TILE)
        for n in which:
            acc = (acc_k, acc_v)[n]
            far_copies(j, half, (n,))[0].wait_recv()
            near_send[j, n, rows, :] = (
                far_in[j, n, rows, :].astype(f32) + acc[j, pl.ds(ROWS + half * TILE, TILE), :]
            ).astype(bf16)
            near_copies(j, half, (n,))[0].start()

    def finish(j, half):
        rows = pl.ds(half * TILE, TILE)
        mine = pl.ds(2 * ROWS + half * TILE, TILE)
        unit, inverse = unit_rows(kcat[j, mine, :])
        near_copies(j, half, (0,))[0].wait_recv()
        grad = (near_in[j, 0, rows, :].astype(f32) + acc_k[j, mine, :]) * score_scale
        turned = grad * cos_table[mine, :] - half_turn(grad) * sin_table[mine, :]
        weighted = turned * key_gain[...]
        mean = jnp.mean(weighted * unit, axis=-1, keepdims=True)
        dk_all[rows, columns(j)] = (inverse * (weighted - unit * mean)).astype(bf16)
        near_copies(j, half, (1,))[0].wait_recv()
        dv_all[rows, columns(j)] = (
            near_in[j, 1, rows, :].astype(f32) + acc_v[j, mine, :]
        ).astype(bf16)

    def between(j):
        @pl.when(j < 3)
        def _():
            relay(j + 1, 1)

        @pl.when(j < 2)
        def _():
            start_own(j + 2, 1)

        @pl.when(j == 0)
        def _():
            start_own(3, 0)

        @pl.when(j >= 1)
        def _():
            hand_on(j - 1, 1, (0,))

        @pl.when((j >= 1) & (j < 3))
        def _():
            hand_on(j - 1, 1, (1,))

        @pl.when(j == 2)
        def _():
            finish(0, 0)
            finish(0, 1)

    def sum_copy(n, k):
        size, mine, place = stages[n]
        return pltpu.make_async_remote_copy(
            src_ref=sum_send.at[n],
            dst_ref=sum_in.at[n, mine],
            send_sem=sum_ssem.at[n, k],
            recv_sem=sum_rsem.at[n, mine],
            device_id=place(lax.rem(mine + k, size)),
            device_id_type=MESH,
        )

    def sum_arrival(n, k):
        size, mine, place = stages[n]
        source = lax.rem(mine + size - k, size)
        return pltpu.make_async_remote_copy(
            src_ref=sum_send.at[n],
            dst_ref=sum_in.at[n, source],
            send_sem=sum_ssem.at[n, k],
            recv_sem=sum_rsem.at[n, source],
            device_id=place(source),
            device_id_type=MESH,
        )

    def start_sum(n, value):
        size, mine, place = stages[n]
        sum_send[n] = value
        sum_in[n, mine] = value
        for k in range(1, size):
            sum_copy(n, k).start()

    def end_sum(n):
        size, mine, place = stages[n]
        for k in range(1, size):
            sum_arrival(n, k).wait_recv()
        value = sum_in[n, 0]
        for k in range(1, size):
            value = value + sum_in[n, k]
        return value

    def gain_part(j):
        def gain_step(n, inner):
            here = pl.ds(pl.multiple_of(n * TILE, TILE), TILE)
            grad = acc_k[j, here, :] * score_scale
            turned = grad * cos_table[here, :] - half_turn(grad) * sin_table[here, :]
            gain_acc[1] += fold_rows(turned * kunit[here, :])
            return inner

        lax.fori_loop(0, KEYS // TILE, gain_step, 0)

    def last_gain(j):
        gain_part(j)
        spread = jnp.where(
            lax.broadcasted_iota(jnp.int32, (8, DIM), 0) == 0,
            jnp.sum(gain_acc[0], axis=0, keepdims=True),
            jnp.sum(gain_acc[1], axis=0, keepdims=True),
        )
        start_sum(0, spread)

    def head_step(j, carry):
        @pl.when(j >= 1)
        def _():
            hand_on(j - 1, 0)

        key_norm(j, ROWS, 2 * ROWS)
        acc_k[j] = jnp.zeros((KEYS, DIM), f32)
        acc_v[j] = jnp.zeros((KEYS, DIM), f32)
        relay_copies(j, (0,))[0].wait_recv()
        key_norm(j, 0, ROWS)

        def row_step(i, inner):
            attend(j, i)

            @pl.when(2 * j + i == 2 * HEADS - 1)
            def _():
                last_gain(j)

            rows = pl.ds(pl.multiple_of(i * TILE, TILE), TILE)
            far_send[j, 0, rows, :] = acc_k[j, rows, :].astype(bf16)
            far_send[j, 1, rows, :] = acc_v[j, rows, :].astype(bf16)
            for copy in far_copies(j, i):
                copy.start()

            @pl.when(i == 0)
            def _():
                between(j)

            return inner

        lax.fori_loop(0, ROWS // TILE, row_step, 0)

        @pl.when(j < 2)
        def _():
            relay(j + 2, 0)

        @pl.when(j < 3)
        def _():
            gain_part(j)

        return carry

    lax.fori_loop(0, HEADS, head_step, 0)

    hand_on(2, 1, (1,))
    hand_on(3, 0)
    finish(1, 0)
    finish(1, 1)
    hand_on(3, 1, (0,))
    start_sum(1, end_sum(0))
    hand_on(3, 1, (1,))
    start_sum(2, end_sum(1))
    finish(2, 0)
    finish(2, 1)
    finish(3, 0)
    gains = end_sum(2)
    query_gain_out[...] = gains[0:1]
    key_gain_out[...] = gains[1:2]
    finish(3, 1)

    for n, (size, mine, place) in enumerate(stages):
        for k in range(1, size):
            sum_copy(n, k).wait_send()

    def drain(j, carry):
        backward = [copy(j, half) for copy in (far_copies, near_copies) for half in range(2)]
        for copies in (own_copies(j), relay_copies(j), *backward):
            for copy in copies:
                copy.wait_send()
        return carry

    lax.fori_loop(0, HEADS, drain, 0)


def write_out(*refs):
    sources, targets, sem = refs[:5], refs[5:10], refs[10]
    copies = [
        pltpu.make_async_copy(src, dst, sem.at[n])
        for n, (src, dst) in enumerate(zip(sources, targets))
    ]
    for copy in copies:
        copy.start()
    for copy in copies:
        copy.wait()


def solution(mesh):
    shards, heads = mesh.shape["seq"], mesh.shape["head"]
    most = max(heads, 8, shards // 8)

    def step(q, k, v, out_grad, query_gain, key_gain, doc_starts, windows):
        inverse_freq = 10000.0 ** (-np.arange(DIM // 2, dtype=np.float64) * (2.0 / DIM))
        inverse_freq = jnp.asarray(np.tile(inverse_freq, 2)[None], f32)
        hbm = pl.BlockSpec(memory_space=pltpu.HBM)
        vmem = pl.BlockSpec(memory_space=pltpu.VMEM)
        smem = pl.BlockSpec(memory_space=pltpu.SMEM)
        results = pl.pallas_call(
            functools.partial(kernel, shards, heads),
            out_shape=(
                pltpu.VMEM(q.shape, bf16),
                pltpu.VMEM(k.shape, bf16),
                pltpu.VMEM(v.shape, bf16),
                pltpu.VMEM((1, DIM), f32),
                pltpu.VMEM((1, DIM), f32),
            ),
            in_specs=[hbm] * 4 + [vmem] * 3 + [smem] * 2,
            out_specs=(vmem,) * 5,
            scratch_shapes=[
                pltpu.VMEM((HEADS, KEYS, DIM), bf16),
                pltpu.VMEM((HEADS, KEYS, DIM), bf16),
                pltpu.VMEM((ROWS, 2 * HEADS * DIM), bf16),
                pltpu.VMEM((ROWS, 2 * HEADS * DIM), bf16),
                pltpu.VMEM((KEYS, DIM), f32),
                pltpu.VMEM((KEYS, DIM), f32),
                pltpu.VMEM((KEYS, DIM), bf16),
                pltpu.VMEM((KEYS, DIM), f32),
                pltpu.VMEM((2 * TILE, DIM), bf16),
                pltpu.VMEM((2 * TILE, DIM), f32),
                pltpu.VMEM((2 * TILE, DIM), f32),
                pltpu.VMEM((2 * TILE, DIM), bf16),
                pltpu.VMEM((2, SPAN, TILE), f32),
                pltpu.VMEM((2, SPAN, TILE), f32),
                pltpu.VMEM((HEADS, KEYS, DIM), f32),
                pltpu.VMEM((HEADS, KEYS, DIM), f32),
                pltpu.VMEM((HEADS, 2, ROWS, DIM), bf16),
                pltpu.VMEM((HEADS, 2, ROWS, DIM), bf16),
                pltpu.VMEM((HEADS, 2, ROWS, DIM), bf16),
                pltpu.VMEM((HEADS, 2, ROWS, DIM), bf16),
                pltpu.VMEM((2, 8, DIM), f32),
                pltpu.VMEM((3, 8, DIM), f32),
                pltpu.VMEM((3, most, 8, DIM), f32),
                pltpu.SemaphoreType.DMA((2 * HEADS + 2,)),
            ]
            + [pltpu.SemaphoreType.DMA((HEADS, 2)) for _ in range(4)]
            + [pltpu.SemaphoreType.DMA((HEADS, 2, 2)) for _ in range(4)]
            + [pltpu.SemaphoreType.DMA((3, most)) for _ in range(2)],
            compiler_params=pltpu.CompilerParams(
                collective_id=0, has_side_effects=True, vmem_limit_bytes=58 * 1024 * 1024
            ),
        )(
            q,
            k,
            v,
            out_grad,
            query_gain[None],
            key_gain[None],
            inverse_freq,
            doc_starts,
            windows,
        )
        dq, dk, dv, dq_gain, dk_gain = pl.pallas_call(
            write_out,
            out_shape=tuple(jax.ShapeDtypeStruct(x.shape, x.dtype) for x in results),
            in_specs=[pl.BlockSpec(memory_space=pl.ANY)] * 5,
            out_specs=(pl.BlockSpec(memory_space=pl.ANY),) * 5,
            scratch_shapes=[pltpu.SemaphoreType.DMA((5,))],
            compiler_params=pltpu.CompilerParams(vmem_limit_bytes=4 * 1024 * 1024),
        )(*results)
        return dq, dk, dv, dq_gain[0], dk_gain[0]

    split = P("seq", "head")
    return jax.shard_map(
        step,
        mesh=mesh,
        in_specs=(split,) * 4 + (P(),) * 4,
        out_specs=(split, split, split, P(), P()),
        check_vma=False,
    )
```
